128 devices in a mesh: ent: 32 (over x, z, y_lo), qry: 4 (over y_hi, core).
Axes of the slice: x: 4, y: 4 (y_hi: 2, y_lo: 2; y = y_hi * 2 + y_lo), z: 4, core: 2. Of those that a mesh axis runs over, the one named last changes fastest.
Arguments:
- ent_emb: bfloat16 [65536, 512], P('ent'), may hold values from -1 to 1
- ent_tan: bfloat16 [65536, 512], P('ent'), may hold values from -0.25 to 0.25
- qry_emb: bfloat16 [4096, 512], P(('qry', 'ent')), may hold values from -6 to 6
- qry_tan: bfloat16 [4096, 512], P(('qry', 'ent')), may hold values from -6 to 6
- tails: int32 [4096, 4], P('qry'), may hold values from 0 to 65535
Outputs:
- ent_gnvp: float32 [65536, 512], P(('ent', 'qry'))
- ent_grad: float32 [65536, 512], P(('ent', 'qry'))
- qry_gnvp: float32 [4096, 512], P(('qry', 'ent'))
- qry_grad: float32 [4096, 512], P(('qry', 'ent'))
The draws below stay inside these ranges and needn't reach their ends.
All inputs are finite; a program needn't handle non-finite values.
Results may differ from the reference program's by a relative error of at most 0.0008.
Values may be sent and summed in bfloat16 or wider, within the bound.
A program may use at most 128 MiB of HBM per device.

```python
import math
import jax
import jax.numpy as jnp
from jax import lax

D = 512
K = 4
QRY_DEV = 32
NE = 65536
NQ = 4096
N_ENT = 32
N_QRY = 4


def sign_pattern(key):
    bits = jax.random.randint(jax.random.fold_in(key, 11), (D,), 0, 2)
    return (2 * bits - 1).astype(jnp.float32)


def draw_ent_emb(key, part):
    signs = sign_pattern(key)
    level = (1.3 - math.log(8.0 / NE)) / (1.25 * D)
    noise_key = jax.random.fold_in(key, 21)
    noise = jnp.clip(jax.random.normal(noise_key, (NE, D), jnp.float32), -4.0, 4.0)
    values = noise / math.sqrt(D) + level * signs[None, :]
    return values.astype(jnp.bfloat16)


def draw_qry_emb(key, part):
    signs = sign_pattern(key)
    noise_key = jax.random.fold_in(key, 31)
    noise = jnp.clip(jax.random.normal(noise_key, (NQ, D), jnp.float32), -4.0, 4.0)
    values = noise - 1.25 * signs[None, :]
    return values.astype(jnp.bfloat16)


def set_ends(array, key, least, high):
    longest = array.shape.index(max(array.shape))
    spots = []
    for shift in (0, 1):
        where = [jax.random.randint(jax.random.fold_in(key, axis), (), 0, length) for axis, length in enumerate(array.shape)]
        where[longest] = (where[longest] + shift) % array.shape[longest]
        spots.append(tuple(where))
    return array.at[spots[0]].set(least).at[spots[1]].set(high)


def block_scale(own_key, shape, split, low, high):
    def one(dim, shards_of):
        steps = jax.random.uniform(jax.random.fold_in(jax.random.fold_in(own_key, 6), dim), (shards_of,), jnp.float32, low / len(split), high / len(split))
        return jnp.repeat(jnp.exp(steps), shape[dim] // shards_of).reshape((-1,) + (1,) * (len(shape) - dim - 1))

    factor_of = one(*split[0])
    for cut in split[1:]:
        factor_of = factor_of * one(*cut)
    return factor_of


def bell_draw(rng, dims, spread, limit, cuts=(), kind=jnp.bfloat16):
    values = jax.random.normal(rng, dims, jnp.float32) * spread
    if len(cuts) > 0:
        values = block_scale(rng, dims, cuts, -0.22, 0.18) * values
    return jnp.clip(values, min=-limit, max=limit).astype(kind)


def setup_inputs(seed: int = 0) -> dict:
    seeds = jax.random.split(jax.random.key(seed), 6)
    return {
        "ent_emb": draw_ent_emb(jax.random.fold_in(seeds[5], 71), 0),
        "ent_tan": bell_draw(seeds[1], (NE, D), D ** -0.5, 0.25, ((0, 32),)),
        "qry_emb": draw_qry_emb(jax.random.fold_in(seeds[5], 71), 0),
        "qry_tan": bell_draw(seeds[3], (NQ, D), 1.0, 6.0, ((0, 128),)),
        "tails": set_ends(jax.random.randint(seeds[4], (NQ, K), 0, NE), jax.random.fold_in(seeds[4], 1), 0, NE - 1).astype(jnp.int32),
    }


def dot_nt(a, b):
    return lax.dot_general(a, b, (((1,), (1,)), ((), ())), preferred_element_type=jnp.float32)


def dot_tn(a, b):
    return lax.dot_general(a, b, (((0,), (0,)), ((), ())), preferred_element_type=jnp.float32)


def weights(queries, qtangent, tail_rows, entities, etangent, ent_ids):
    score = dot_nt(queries, entities)
    dscore = dot_nt(qtangent, entities) + dot_nt(queries, etangent)
    prob = jax.nn.sigmoid(score)
    label = jnp.zeros(score.shape, jnp.float32)
    for k in range(tail_rows.shape[1]):
        label = jnp.maximum(label, (tail_rows[:, k:k + 1] == ent_ids[None, :]).astype(jnp.float32))
    ugrad = (prob - label).astype(jnp.bfloat16)
    uhess = (prob * (1.0 - prob) * dscore).astype(jnp.bfloat16)
    return uhess, ugrad


def reference(ent_emb, ent_tan, qry_emb, qry_tan, tails):
    num_ent = ent_emb.shape[0]
    width = ent_emb.shape[1]
    ent_ids = jnp.arange(num_ent, dtype=jnp.int32)
    block = QRY_DEV
    q_all = qry_emb.reshape(N_QRY * N_ENT, block, width)
    dq_all = qry_tan.reshape(N_QRY * N_ENT, block, width)
    t_all = tails.reshape(N_QRY * N_ENT, block, tails.shape[1])

    def one_block(partial_value, ys):
        queries, qtangent, tail_rows = ys
        uhess, ugrad = weights(queries, qtangent, tail_rows, ent_emb, ent_tan, ent_ids)
        qrows = jnp.concatenate([jnp.dot(uhess, ent_emb, preferred_element_type=jnp.float32),
                                 jnp.dot(ugrad, ent_emb, preferred_element_type=jnp.float32)], axis=1)
        add = jnp.concatenate([dot_tn(uhess, queries), dot_tn(ugrad, queries)], axis=1)
        return partial_value + add, qrows

    total, qrows = lax.scan(one_block, jnp.zeros((num_ent, 2 * width), jnp.float32), (q_all, dq_all, t_all))
    qrows = qrows.reshape(-1, 2 * width)
    return total[:, :width], total[:, width:], qrows[:, :width], qrows[:, width:]
```

```python
import jax
import jax.numpy as jnp
from jax import lax
from jax.experimental import pallas as pl
from jax.experimental.pallas import tpu as pltpu
from jax.sharding import PartitionSpec as P

MESH = pl.DeviceIdType.MESH
F32 = jnp.float32
BF16 = jnp.bfloat16
I32 = jnp.int32
I16 = jnp.int16
D = 512
PLANE = 256
SUB = 512
NEAR_FIRST = (1, 3, 2)
GNVP, GRAD = 0, 1

A_Y, A_X0, A_X1, A_Z0, A_Z1, A_ZZ, A_XX, A_N = 0, 2, 6, 10, 14, 18, 34, 50


def dot_nt(a, b):
    return lax.dot_general(a, b, (((1,), (1,)), ((), ())), preferred_element_type=F32)


def dot_tn(a, b):
    return lax.dot_general(a, b, (((0,), (0,)), ((), ())), preferred_element_type=F32)


def dot_nn(a, b):
    return lax.dot_general(a, b, (((1,), (0,)), ((), ())), preferred_element_type=F32)


def quantize(value, code_ref, scale_ref):
    top = jnp.max(jnp.abs(value), axis=(0, 1), keepdims=True)
    top = jnp.maximum(top, 1e-30)
    code_ref[...] = jnp.round(value * (32767.0 / top)).astype(I32).astype(I16)
    scale_ref[...] = jnp.broadcast_to(top * (1.0 / 32767.0), (8, 128))


def dequantize(code_ref, scale_ref):
    return code_ref[...].astype(I32).astype(F32) * scale_ref[0:1, 0:1]


def kernel(
    ent_hbm,
    ett_hbm,
    q_hbm,
    dq_hbm,
    tails_hbm,
    oeh,
    oeg,
    oqh,
    oqg,
    ent,
    ett,
    qp,
    dqp,
    tails,
    tb,
    w,
    qacc,
    eacc,
    drecv,
    csend,
    crecv,
    cssend,
    csrecv,
    b1s,
    b1r,
    b1ss,
    b1sr,
    b2s,
    b2r,
    b2ss,
    b2sr,
    b3s,
    b3r,
    lsem,
    asend,
    arecv,
    dsend,
    drsem,
    cs_sem,
    cr_sem,
    css_sem,
    csr_sem,
    b1s_sem,
    b1r_sem,
    b1ss_sem,
    b1sr_sem,
    b2s_sem,
    b2r_sem,
    b2ss_sem,
    b2sr_sem,
    b3s_sem,
    b3r_sem,
):
    e_idx = lax.axis_index("ent")
    q_idx = lax.axis_index("qry")
    x, z, yl = e_idx // 8, (e_idx // 2) % 4, e_idx % 2
    yh, c = q_idx // 2, q_idx % 2

    def at(xx, zz, yy):
        return ((xx * 4 + zz) * 2 + yy, q_idx)

    def px(d):
        return at((x + d) % 4, z, yl)

    def pz(d):
        return at(x, (z + d) % 4, yl)

    py = at(x, z, 1 - yl)
    pcore = (e_idx, yh * 2 + 1 - c)
    phi = (e_idx, (1 - yh) * 2 + c)

    started = []

    def send(src, dst, ss, rs, peer):
        cp = pltpu.make_async_remote_copy(
            src_ref=src, dst_ref=dst, send_sem=ss, recv_sem=rs, device_id=peer, device_id_type=MESH
        )
        cp.start()
        started.append(cp)

    def arrived(dst, ss, rs):
        pltpu.make_async_remote_copy(
            src_ref=dst, dst_ref=dst, send_sem=ss, recv_sem=rs, device_id=py, device_id_type=MESH
        ).wait_recv()

    def rows(start, size, step):
        return pl.ds(pl.multiple_of(start, step), size)

    barrier = pltpu.get_barrier_semaphore()
    for peer in [px(d) for d in (1, 2, 3)] + [pz(d) for d in (1, 2, 3)] + [py, pcore, phi]:
        pl.semaphore_signal(barrier, inc=1, device_id=peer, device_id_type=MESH)

    panel = (qp, dqp)
    own = (q_hbm, dq_hbm)
    my16 = [rows(h * 128 + x * 32 + yl * 16, 16, 16) for h in (0, 1)]
    his16 = [rows(h * 128 + x * 32 + (1 - yl) * 16, 16, 16) for h in (0, 1)]

    local = []
    for a in (0, 1):
        for h in (0, 1):
            cp = pltpu.make_async_copy(
                own[a].at[pl.ds(h * 16, 16)], panel[a].at[z, my16[h]], lsem.at[a * 2 + h]
            )
            cp.start()
            local.append(cp)
    for i, (src, dst) in enumerate(((tails_hbm, tails), (ent_hbm, ent), (ett_hbm, ett))):
        cp = pltpu.make_async_copy(src, dst, lsem.at[4 + i])
        cp.start()
        local.append(cp)
    for cp in local[:4]:
        cp.wait()
    pl.semaphore_wait(barrier, 9)

    def slot(a, i):
        return asend.at[a, i], arecv.at[a, i]

    def first_sends(a):
        for h in (0, 1):
            here = panel[a].at[z, my16[h]]
            send(here, here, *slot(a, A_Y + h), py)
        for d in NEAR_FIRST:
            here = panel[a].at[z, my16[0]]
            send(here, here, *slot(a, A_X0 + d), px(d))
            here = panel[a].at[z, my16[1]]
            send(here, here, *slot(a, A_Z0 + d), pz(d))

    def relay_z(a, j):
        here = panel[a].at[z, rows(((x + j) % 4) * 32, 32, 32)]
        for d in NEAR_FIRST:
            send(here, here, *slot(a, A_ZZ + j * 4 + d), pz(d))

    def relay_x(a, j):
        here = panel[a].at[(z + j) % 4, rows(128 + x * 32, 32, 32)]
        for d in NEAR_FIRST:
            send(here, here, *slot(a, A_XX + j * 4 + d), px(d))

    def second_sends(a):
        for h in (0, 1):
            arrived(panel[a].at[z, his16[h]], *slot(a, A_Y + h))
        for d in NEAR_FIRST:
            here = panel[a].at[z, his16[0]]
            send(here, here, *slot(a, A_X1 + d), px(d))
            here = panel[a].at[z, his16[1]]
            send(here, here, *slot(a, A_Z1 + d), pz(d))
        relay_z(a, 0)
        relay_x(a, 0)

    def relays(a):
        for d in NEAR_FIRST:
            for k in (0, 1):
                there = panel[a].at[z, rows(((x - d + 4) % 4) * 32 + k * 16, 16, 16)]
                arrived(there, *slot(a, (A_X0, A_X1)[k] + d))
            relay_z(a, (4 - d) % 4)
            for k in (0, 1):
                there = panel[a].at[(z - d + 4) % 4, rows(128 + x * 32 + k * 16, 16, 16)]
                arrived(there, *slot(a, (A_Z0, A_Z1)[k] + d))
            relay_x(a, (4 - d) % 4)

    def plane_arrived(a, j):
        p = (z + j) % 4
        if j:
            for i in range(4):
                there = panel[a].at[p, rows(((x + i) % 4) * 32, 32, 32)]
                arrived(there, *slot(a, A_ZZ + i * 4 + (4 - j)))
        for d in NEAR_FIRST:
            there = panel[a].at[p, rows(128 + ((x - d + 4) % 4) * 32, 32, 32)]
            arrived(there, *slot(a, A_XX + j * 4 + d))

    first_sends(0)
    first_sends(1)

    def clear(i, _):
        eacc[0, rows(i * 128, 128, 128)] = jnp.zeros((128, D), F32)
        eacc[1, rows(i * 128, 128, 128)] = jnp.zeros((128, D), F32)
        return 0

    lax.fori_loop(0, 16, clear, 0)
    second_sends(0)

    local[4].wait()

    def spread(i, _):
        xx, zz, yy = i // 8, (i // 2) % 4, i % 2
        for h in (0, 1):
            t = tails[rows(i * 32 + h * 16, 16, 16)] - e_idx * (4 * SUB)
            for k in range(4):
                tb[k, zz, rows(h * 128 + xx * 32 + yy * 16, 16, 16)] = jnp.broadcast_to(
                    t[:, k : k + 1], (16, 128)
                )
        return 0

    lax.fori_loop(0, 32, spread, 0)

    def clear_q(i, _):
        qacc[0, i] = jnp.zeros((PLANE, D), F32)
        qacc[1, i] = jnp.zeros((PLANE, D), F32)
        return 0

    lax.fori_loop(0, 4, clear_q, 0)
    relays(0)
    second_sends(1)
    local[5].wait()

    def grad_tile(p, s):
        es = rows(s * SUB, SUB, SUB)
        q = qp[p]
        e = ent[es]
        score = dot_nt(q, e)
        lane = lax.broadcasted_iota(I32, (PLANE, 128), 1)
        label = []
        for b in range(SUB // 128):
            ids = lane + (s * SUB + b * 128)
            hit = tb[0, p] == ids
            for k in range(1, 4):
                hit = hit | (tb[k, p] == ids)
            label.append(jnp.where(hit, 1.0, 0.0).astype(F32))
        label = jnp.concatenate(label, axis=1)
        prob = 1.0 / (1.0 + jnp.exp(-score))
        w[p, s] = prob * (1.0 - prob)
        ugrad = (prob - label).astype(BF16)
        qacc[GRAD, p] += dot_nn(ugrad, e)
        eacc[GRAD, es] += dot_tn(ugrad, q)

    def gnvp_tile(p, s):
        es = rows(s * SUB, SUB, SUB)
        q = qp[p]
        e = ent[es]
        dscore = dot_nt(dqp[p], e) + dot_nt(q, ett[es])
        uhess = (w[p, s] * dscore).astype(BF16)
        qacc[GNVP, p] += dot_nn(uhess, e)
        eacc[GNVP, es] += dot_tn(uhess, q)

    far_other = (1 - yh) * 2 + 1 - c
    far_same = (1 - yh) * 2 + c
    near_other = yh * 2 + 1 - c
    near_same = yh * 2 + c

    def both(tile, j, far):
        p = (z + j) % 4
        base = (1 - yh if far else yh) * 2

        def step(i, _):
            tile(p, base + (1 - c + i) % 2)
            return 0

        lax.fori_loop(0, 2, step, 0)

    def to_core(k, i, s):
        for b in (0, 1):
            send(
                eacc.at[k, rows(s * SUB + b * 256, 256, 256)],
                drecv.at[k, i, pl.ds(b * 256, 256)],
                dsend.at[k, i, b],
                drsem.at[k, i, b],
                pcore,
            )

    def to_far(k):
        for b in (0, 1):
            here = drecv.at[k, 0, pl.ds(b * 256, 256)]
            arrived(here, dsend.at[k, 0, b], drsem.at[k, 0, b])
            value = eacc[k, rows(far_same * SUB + b * 256, 256, 256)] + here[...]
            quantize(value, csend.at[k, b], cssend.at[k, b])
            send(csend.at[k, b], crecv.at[k, b], cs_sem.at[k, b], cr_sem.at[k, b], phi)
            send(cssend.at[k, b], csrecv.at[k, b], css_sem.at[k, b], csr_sem.at[k, b], phi)

    def finish_entities(k, out):
        for b in (0, 1):
            here = drecv.at[k, 1, pl.ds(b * 256, 256)]
            arrived(here, dsend.at[k, 1, b], drsem.at[k, 1, b])
            arrived(csrecv.at[k, b], css_sem.at[k, b], csr_sem.at[k, b])
            arrived(crecv.at[k, b], cs_sem.at[k, b], cr_sem.at[k, b])
            out[pl.ds(b * 256, 256)] = (
                eacc[k, rows(near_same * SUB + b * 256, 256, 256)]
                + here[...]
                + dequantize(crecv.at[k, b], csrecv.at[k, b])
            )

    def to_1(k, d, value, peer):
        i = d - 1
        quantize(value, b1s.at[k, i], b1ss.at[k, i])
        send(b1ss.at[k, i], b1sr.at[k, i], b1ss_sem.at[k, i], b1sr_sem.at[k, i], peer)
        send(b1s.at[k, i], b1r.at[k, i], b1s_sem.at[k, i], b1r_sem.at[k, i], peer)

    def of_1(k, i):
        arrived(b1sr.at[k, i], b1ss_sem.at[k, i], b1sr_sem.at[k, i])
        arrived(b1r.at[k, i], b1s_sem.at[k, i], b1r_sem.at[k, i])
        return dequantize(b1r.at[k, i], b1sr.at[k, i])

    def to_2(k, d, value, peer):
        i = d - 1
        quantize(value, b2s.at[k, i], b2ss.at[k, i])
        send(b2ss.at[k, i], b2sr.at[k, i], b2ss_sem.at[k, i], b2sr_sem.at[k, i], peer)
        send(b2s.at[k, i], b2r.at[k, i], b2s_sem.at[k, i], b2r_sem.at[k, i], peer)

    def of_2(k, i):
        arrived(b2sr.at[k, i], b2ss_sem.at[k, i], b2sr_sem.at[k, i])
        arrived(b2r.at[k, i], b2s_sem.at[k, i], b2r_sem.at[k, i])
        return dequantize(b2r.at[k, i], b2sr.at[k, i])

    def column(k, p, xx):
        return jnp.concatenate([qacc[k, p, rows(h * 128 + xx * 32, 32, 32)] for h in (0, 1)], axis=0)

    def to_3(k, total):
        b3s[k] = total
        for h in (0, 1):
            send(
                b3s.at[k, rows(h * 32 + (1 - yl) * 16, 16, 16)],
                b3r.at[k, pl.ds(h * 16, 16)],
                b3s_sem.at[k, h],
                b3r_sem.at[k, h],
                py,
            )

    def finish_queries(k, out):
        for h in (0, 1):
            arrived(b3r.at[k, pl.ds(h * 16, 16)], b3s_sem.at[k, h], b3r_sem.at[k, h])
            out[pl.ds(h * 16, 16)] = b3s[k, rows(h * 32 + yl * 16, 16, 16)] + b3r[k, pl.ds(h * 16, 16)]

    for j in (0, 1, 3):
        plane_arrived(0, j)
        both(grad_tile, j, True)
    plane_arrived(0, 2)
    grad_tile((z + 2) % 4, far_other)
    to_core(GRAD, 0, far_other)
    grad_tile((z + 2) % 4, far_same)
    relays(1)
    both(grad_tile, 0, False)
    to_far(GRAD)

    def near_grad(i, _):
        p = (z + i) % 4
        grad_tile(p, near_other)
        grad_tile(p, near_same)
        return 0

    lax.fori_loop(1, 4, near_grad, 0)
    to_core(GRAD, 1, near_other)
    for d in NEAR_FIRST:
        value = jnp.concatenate([column(GRAD, p, (x + d) % 4) for p in range(4)], axis=0)
        to_1(GRAD, d, value, px(d))
    local[6].wait()
    for j in (0, 1, 3):
        plane_arrived(1, j)
        both(gnvp_tile, j, True)
    plane_arrived(1, 2)
    gnvp_tile((z + 2) % 4, far_other)
    to_core(GNVP, 0, far_other)
    gnvp_tile((z + 2) % 4, far_same)
    both(gnvp_tile, 1, False)
    to_far(GNVP)
    to_1(GNVP, 1, qacc[GNVP, (z + 1) % 4], pz(1))
    both(gnvp_tile, 3, False)
    to_1(GNVP, 3, qacc[GNVP, (z + 3) % 4], pz(3))
    both(gnvp_tile, 2, False)
    to_1(GNVP, 2, qacc[GNVP, (z + 2) % 4], pz(2))
    total = jnp.concatenate([column(GRAD, p, x) for p in range(4)], axis=0)
    for i in range(3):
        total = total + of_1(GRAD, i)
    for p in range(4):
        w[0, far_same, pl.ds(p * 64, 64)] = total[p * 64 : (p + 1) * 64]
    for d in NEAR_FIRST:
        to_2(GRAD, d, w[0, far_same, rows(((z + d) % 4) * 64, 64, 64)], pz(d))
    both(gnvp_tile, 0, False)
    to_core(GNVP, 1, near_other)
    total = qacc[GNVP, z]
    for i in range(3):
        total = total + of_1(GNVP, i)
    qacc[GNVP, z] = total
    for d in NEAR_FIRST:
        to_2(GNVP, d, column(GNVP, z, (x + d) % 4), px(d))
    total = w[0, far_same, rows(z * 64, 64, 64)]
    for i in range(3):
        total = total + of_2(GRAD, i)
    to_3(GRAD, total)
    total = column(GNVP, z, x)
    for i in range(3):
        total = total + of_2(GNVP, i)
    to_3(GNVP, total)
    finish_queries(GRAD, oqg)
    finish_queries(GNVP, oqh)
    finish_entities(GRAD, oeg)
    finish_entities(GNVP, oeh)
    for cp in started:
        cp.wait_send()


def per_device(ent_emb, ent_tan, qry_emb, qry_tan, tails):
    any_space = pl.BlockSpec(memory_space=pl.ANY)
    vmem = pl.BlockSpec(memory_space=pltpu.VMEM)
    dma = pltpu.SemaphoreType.DMA
    outs = (
        jax.ShapeDtypeStruct((SUB, D), F32),
        jax.ShapeDtypeStruct((SUB, D), F32),
        jax.ShapeDtypeStruct((32, D), F32),
        jax.ShapeDtypeStruct((32, D), F32),
    )
    return pl.pallas_call(
        kernel,
        out_shape=outs,
        in_specs=[any_space] * 5,
        out_specs=[vmem] * 4,
        scratch_shapes=[
            pltpu.VMEM((4 * SUB, D), BF16),
            pltpu.VMEM((4 * SUB, D), BF16),
            pltpu.VMEM((4, PLANE, D), BF16),
            pltpu.VMEM((4, PLANE, D), BF16),
            pltpu.VMEM((4 * PLANE, 4), I32),
            pltpu.VMEM((4, 4, PLANE, 128), I32),
            pltpu.VMEM((4, 4, PLANE, SUB), F32),
            pltpu.VMEM((2, 4, PLANE, D), F32),
            pltpu.VMEM((2, 4 * SUB, D), F32),
            pltpu.VMEM((2, 2, SUB, D), F32),
            pltpu.VMEM((2, 2, 256, D), I16),
            pltpu.VMEM((2, 2, 256, D), I16),
            pltpu.VMEM((2, 2, 8, 128), F32),
            pltpu.VMEM((2, 2, 8, 128), F32),
            pltpu.VMEM((2, 3, PLANE, D), I16),
            pltpu.VMEM((2, 3, PLANE, D), I16),
            pltpu.VMEM((2, 3, 8, 128), F32),
            pltpu.VMEM((2, 3, 8, 128), F32),
            pltpu.VMEM((2, 3, 64, D), I16),
            pltpu.VMEM((2, 3, 64, D), I16),
            pltpu.VMEM((2, 3, 8, 128), F32),
            pltpu.VMEM((2, 3, 8, 128), F32),
            pltpu.VMEM((2, 64, D), F32),
            pltpu.VMEM((2, 32, D), F32),
            dma((7,)),
            dma((2, A_N)),
            dma((2, A_N)),
            dma((2, 2, 2)),
            dma((2, 2, 2)),
            dma((2, 2)),
            dma((2, 2)),
            dma((2, 2)),
            dma((2, 2)),
            dma((2, 3)),
            dma((2, 3)),
            dma((2, 3)),
            dma((2, 3)),
            dma((2, 3)),
            dma((2, 3)),
            dma((2, 3)),
            dma((2, 3)),
            dma((2, 2)),
            dma((2, 2)),
        ],
        compiler_params=pltpu.CompilerParams(
            collective_id=0, has_side_effects=True, vmem_limit_bytes=60 * 2**20
        ),
    )(ent_emb, ent_tan, qry_emb, qry_tan, tails)


def solution(mesh):
    return jax.shard_map(
        per_device,
        mesh=mesh,
        in_specs=(
            P("ent", None),
            P("ent", None),
            P(("qry", "ent"), None),
            P(("qry", "ent"), None),
            P("qry", None),
        ),
        out_specs=(
            P(("ent", "qry"), None),
            P(("ent", "qry"), None),
            P(("qry", "ent"), None),
            P(("qry", "ent"), None),
        ),
        check_vma=False,
    )
```

```python
import jax
import jax.numpy as jnp
from jax import lax
from jax.experimental import pallas as pl
from jax.experimental.pallas import tpu as pltpu
from jax.sharding import PartitionSpec as P

MESH = pl.DeviceIdType.MESH
F32 = jnp.float32
BF16 = jnp.bfloat16
I32 = jnp.int32
I16 = jnp.int16
D = 512
PLANE = 256
SUB = 512
NEAR_FIRST = (1, 3, 2)
VMEM_LIMIT = 50 * 2**20
GNVP, GRAD = 0, 1

A_X, A_Z, A_ZZ, A_XX, A_N = 0, 8, 16, 32, 48


def dot_nt(a, b):
    return lax.dot_general(a, b, (((1,), (1,)), ((), ())), preferred_element_type=F32)


def dot_tn(a, b):
    return lax.dot_general(a, b, (((0,), (0,)), ((), ())), preferred_element_type=F32)


def dot_nn(a, b):
    return lax.dot_general(a, b, (((1,), (0,)), ((), ())), preferred_element_type=F32)


def quantize(value, code_ref, scale_ref):
    top = jnp.max(jnp.abs(value), axis=(0, 1), keepdims=True)
    top = jnp.maximum(top, 1e-30)
    code_ref[...] = jnp.round(value * (32767.0 / top)).astype(I32).astype(I16)
    scale_ref[...] = jnp.broadcast_to(top * (1.0 / 32767.0), (8, 128))


def dequantize(code_ref, scale_ref):
    return code_ref[...].astype(I32).astype(F32) * scale_ref[0:1, 0:1]


def kernel(
    ent_hbm,
    ett_hbm,
    q_hbm,
    dq_hbm,
    tails_hbm,
    oeh,
    oeg,
    oqh,
    oqg,
    ent,
    ett,
    qp,
    dqp,
    tails,
    tb,
    w,
    qacc,
    eacc,
    drecv,
    csend,
    crecv,
    cssend,
    csrecv,
    bq,
    bqs,
    br0,
    br0s,
    br1,
    br1s,
    b2s,
    b2r,
    b3s,
    b3r,
    lsem,
    asend,
    arecv,
    dsend,
    drsem,
    cs_sem,
    cr_sem,
    css_sem,
    csr_sem,
    b0_ss,
    b0_rs,
    b0s_ss,
    b0s_rs,
    b1_ss,
    b1_rs,
    b1s_ss,
    b1s_rs,
    b2_ss,
    b2_rs,
    b3_ss,
    b3_rs,
):
    e_idx = lax.axis_index("ent")
    q_idx = lax.axis_index("qry")
    x, z, yl = e_idx // 8, (e_idx // 2) % 4, e_idx % 2
    yh, c = q_idx // 2, q_idx % 2

    def at(xx, zz, yy):
        return ((xx * 4 + zz) * 2 + yy, q_idx)

    def px(d, dy=0):
        return at((x + d) % 4, z, (yl + dy) % 2)

    def pz(d, dy=0):
        return at(x, (z + d) % 4, (yl + dy) % 2)

    py = at(x, z, 1 - yl)
    pcore = (e_idx, yh * 2 + 1 - c)
    phi = (e_idx, (1 - yh) * 2 + c)

    started = []

    def send(src, dst, ss, rs, peer):
        cp = pltpu.make_async_remote_copy(
            src_ref=src, dst_ref=dst, send_sem=ss, recv_sem=rs, device_id=peer, device_id_type=MESH
        )
        cp.start()
        started.append(cp)

    def arrived(dst, ss, rs):
        pltpu.make_async_remote_copy(
            src_ref=dst, dst_ref=dst, send_sem=ss, recv_sem=rs, device_id=py, device_id_type=MESH
        ).wait_recv()

    def rows(start, size, step):
        return pl.ds(pl.multiple_of(start, step), size)

    barrier = pltpu.get_barrier_semaphore()
    sides = [(d, dy) for d in (1, 2, 3) for dy in (0, 1)]
    for peer in [px(*s) for s in sides] + [pz(*s) for s in sides] + [py, pcore, phi]:
        pl.semaphore_signal(barrier, inc=1, device_id=peer, device_id_type=MESH)

    panel = (qp, dqp)
    own = (q_hbm, dq_hbm)
    my16 = [rows(h * 128 + x * 32 + yl * 16, 16, 16) for h in (0, 1)]

    local = []
    for a in (0, 1):
        for h in (0, 1):
            cp = pltpu.make_async_copy(
                own[a].at[pl.ds(h * 16, 16)], panel[a].at[z, my16[h]], lsem.at[a * 2 + h]
            )
            cp.start()
            local.append(cp)
    for i, (src, dst) in enumerate(((tails_hbm, tails), (ent_hbm, ent), (ett_hbm, ett))):
        cp = pltpu.make_async_copy(src, dst, lsem.at[4 + i])
        cp.start()
        local.append(cp)
    for cp in local[:4]:
        cp.wait()
    pl.semaphore_wait(barrier, 15)

    def slot(a, i):
        return asend.at[a, i], arecv.at[a, i]

    def first_sends(a):
        here = [panel[a].at[z, my16[h]] for h in (0, 1)]
        send(here[0], here[0], *slot(a, A_X + 1), py)
        send(here[1], here[1], *slot(a, A_Z + 1), py)
        for d in NEAR_FIRST:
            for dy in (0, 1):
                send(here[0], here[0], *slot(a, A_X + d * 2 + dy), px(d, dy))
                send(here[1], here[1], *slot(a, A_Z + d * 2 + dy), pz(d, dy))

    def first_arrived(a, d):
        for dy in (0, 1) if d else (1,):
            k = (yl + dy) % 2 * 16
            there = panel[a].at[z, rows(((x - d + 4) % 4) * 32 + k, 16, 16)]
            arrived(there, *slot(a, A_X + d * 2 + dy))
            there = panel[a].at[(z - d + 4) % 4, rows(128 + x * 32 + k, 16, 16)]
            arrived(there, *slot(a, A_Z + d * 2 + dy))

    def relays(a):
        for d in (0,) + NEAR_FIRST:
            first_arrived(a, d)
            j = (4 - d) % 4
            here = panel[a].at[z, rows(((x + j) % 4) * 32, 32, 32)]
            for e in NEAR_FIRST:
                send(here, here, *slot(a, A_ZZ + j * 4 + e), pz(e))
            here = panel[a].at[(z + j) % 4, rows(128 + x * 32, 32, 32)]
            for e in NEAR_FIRST:
                send(here, here, *slot(a, A_XX + j * 4 + e), px(e))

    def plane_arrived(a, j):
        p = (z + j) % 4
        if j:
            for i in range(4):
                there = panel[a].at[p, rows(((x + i) % 4) * 32, 32, 32)]
                arrived(there, *slot(a, A_ZZ + i * 4 + (4 - j)))
        for d in NEAR_FIRST:
            there = panel[a].at[p, rows(128 + ((x - d + 4) % 4) * 32, 32, 32)]
            arrived(there, *slot(a, A_XX + j * 4 + d))

    first_sends(0)
    first_sends(1)

    local[4].wait()

    def spread(m, _):
        for k in range(4):
            t = tails[pl.ds(k, 1), pl.ds(pl.multiple_of(m * 128, 128), 128)] - e_idx * (4 * SUB)
            t = jnp.broadcast_to(t, (128, 128)).T
            for i in range(8):
                to = rows(i % 2 * 128 + m // 2 * 32 + i // 2 % 2 * 16, 16, 16)
                tb[k, m % 2 * 2 + i // 4, to] = t[i * 16 : (i + 1) * 16]
        return 0

    lax.fori_loop(0, 8, spread, 0)
    relays(0)
    relays(1)
    local[5].wait()

    def add(ref, value, first):
        ref[...] = value if first else ref[...] + value

    def grad_tile(j, far, first):
        p = (z + j) % 4
        half = 1 - yh if far else yh
        es = rows(half * 2 * SUB, 2 * SUB, 2 * SUB)
        q = qp[p]
        e = ent[es]
        score = dot_nt(q, e)
        lane = lax.broadcasted_iota(I32, (PLANE, 128), 1)
        label = []
        for b in range(2 * SUB // 128):
            ids = lane + (half * 2 * SUB + b * 128)
            hit = tb[0, p] == ids
            for k in range(1, 4):
                hit = hit | (tb[k, p] == ids)
            label.append(jnp.where(hit, 1.0, 0.0).astype(F32))
        label = jnp.concatenate(label, axis=1)
        prob = 1.0 / (1.0 + jnp.exp(-score))
        w[half, p] = prob * (1.0 - prob)
        ugrad = (prob - label).astype(BF16)
        add(qacc.at[GRAD, p], dot_nn(ugrad, e), far)
        add(eacc.at[GRAD, es], dot_tn(ugrad, q), first)

    def gnvp_tile(j, far, first):
        p = (z + j) % 4
        half = 1 - yh if far else yh
        es = rows(half * 2 * SUB, 2 * SUB, 2 * SUB)
        q = qp[p]
        e = ent[es]
        dscore = dot_nt(
            jnp.concatenate([dqp[p], q], axis=1), jnp.concatenate([e, ett[es]], axis=1)
        )
        uhess = (w[half, p] * dscore).astype(BF16)
        add(qacc.at[GNVP, p], dot_nn(uhess, e), far)
        add(eacc.at[GNVP, es], dot_tn(uhess, q), first)

    far_other = (1 - yh) * 2 + 1 - c
    far_same = (1 - yh) * 2 + c
    near_other = yh * 2 + 1 - c
    near_same = yh * 2 + c

    def to_core(k, i, s):
        for b in (0, 1):
            send(
                eacc.at[k, rows(s * SUB + b * 256, 256, 256)],
                drecv.at[k, i, pl.ds(b * 256, 256)],
                dsend.at[k, i, b],
                drsem.at[k, i, b],
                pcore,
            )

    def to_far(k):
        for b in (0, 1):
            here = drecv.at[k, 0, pl.ds(b * 256, 256)]
            arrived(here, dsend.at[k, 0, b], drsem.at[k, 0, b])
            value = eacc[k, rows(far_same * SUB + b * 256, 256, 256)] + here[...]
            quantize(value, csend.at[k, b], cssend.at[k, b])
            send(csend.at[k, b], crecv.at[k, b], cs_sem.at[k, b], cr_sem.at[k, b], phi)
            send(cssend.at[k, b], csrecv.at[k, b], css_sem.at[k, b], csr_sem.at[k, b], phi)

    def finish_entities(k, out):
        for b in (0, 1):
            here = drecv.at[k, 1, pl.ds(b * 256, 256)]
            arrived(here, dsend.at[k, 1, b], drsem.at[k, 1, b])
            arrived(csrecv.at[k, b], css_sem.at[k, b], csr_sem.at[k, b])
            arrived(crecv.at[k, b], cs_sem.at[k, b], cr_sem.at[k, b])
            out[pl.ds(b * 256, 256)] = (
                eacc[k, rows(near_same * SUB + b * 256, 256, 256)]
                + here[...]
                + dequantize(crecv.at[k, b], csrecv.at[k, b])
            )

    def to_1(k, j):
        p = (z + j) % 4
        quantize(qacc[k, p], bq.at[k, j], bqs.at[k, j])
        if j:
            send(bqs.at[k, j], br0s.at[k, j], b0s_ss.at[k, j], b0s_rs.at[k, j], pz(j))
            here = bq.at[k, j, pl.ds(0, 128)]
            send(here, br0.at[k, j], b0_ss.at[k, j], b0_rs.at[k, j], pz(j))
        for d in NEAR_FIRST:
            send(bqs.at[k, j], br1s.at[k, j, d], b1s_ss.at[k, j, d], b1s_rs.at[k, j, d], px(d))
            here = bq.at[k, j, rows(128 + ((x + d) % 4) * 32, 32, 32)]
            send(here, br1.at[k, j, d], b1_ss.at[k, j, d], b1_rs.at[k, j, d], px(d))

    def to_2(k):
        total = qacc[k, z, pl.ds(0, 128)]
        for j in NEAR_FIRST:
            arrived(br0s.at[k, j], b0s_ss.at[k, j], b0s_rs.at[k, j])
            arrived(br0.at[k, j], b0_ss.at[k, j], b0_rs.at[k, j])
            total = total + dequantize(br0.at[k, j], br0s.at[k, j])
        b2s[k, 0] = total
        for d in NEAR_FIRST:
            here = b2s.at[k, 0, rows(((x + d) % 4) * 32, 32, 32)]
            send(here, b2r.at[k, d], b2_ss.at[k, d], b2_rs.at[k, d], px(d))
        for j in (2, 1, 3, 0):
            total = qacc[k, (z + j) % 4, rows(128 + x * 32, 32, 32)]
            for d in NEAR_FIRST:
                arrived(br1s.at[k, j, d], b1s_ss.at[k, j, d], b1s_rs.at[k, j, d])
                arrived(br1.at[k, j, d], b1_ss.at[k, j, d], b1_rs.at[k, j, d])
                total = total + dequantize(br1.at[k, j, d], br1s.at[k, j, d])
            b2s[k, 1, pl.ds(j * 32, 32)] = total
            if j:
                here = b2s.at[k, 1, pl.ds(j * 32, 32)]
                send(here, b2r.at[k, 4 + j], b2_ss.at[k, 4 + j], b2_rs.at[k, 4 + j], pz(j))

    def to_3(k):
        for h in (0, 1):
            total = b2s[k, 0, rows(x * 32, 32, 32)] if h == 0 else b2s[k, 1, pl.ds(0, 32)]
            for d in NEAR_FIRST:
                i = h * 4 + d
                arrived(b2r.at[k, i], b2_ss.at[k, i], b2_rs.at[k, i])
                total = total + b2r[k, i]
            b3s[k, h] = total
            here = b3s.at[k, h, rows((1 - yl) * 16, 16, 16)]
            send(here, b3r.at[k, h], b3_ss.at[k, h], b3_rs.at[k, h], py)

    def finish_queries(k, out):
        for h in (0, 1):
            arrived(b3r.at[k, h], b3_ss.at[k, h], b3_rs.at[k, h])
            out[pl.ds(h * 16, 16)] = b3s[k, h, rows(yl * 16, 16, 16)] + b3r[k, h]

    for j in (0,) + NEAR_FIRST:
        plane_arrived(0, j)
        grad_tile(j, True, j == 0)
    to_core(GRAD, 0, far_other)
    grad_tile(2, False, True)
    to_1(GRAD, 2)
    grad_tile(1, False, False)
    to_far(GRAD)
    to_1(GRAD, 1)
    grad_tile(3, False, False)
    to_1(GRAD, 3)
    grad_tile(0, False, False)
    to_1(GRAD, 0)
    to_core(GRAD, 1, near_other)
    local[6].wait()
    for j in (0,) + NEAR_FIRST:
        plane_arrived(1, j)
        gnvp_tile(j, True, j == 0)
    to_core(GNVP, 0, far_other)
    gnvp_tile(2, False, True)
    to_1(GNVP, 2)
    gnvp_tile(1, False, False)
    to_far(GNVP)
    to_1(GNVP, 1)
    to_2(GRAD)
    gnvp_tile(3, False, False)
    to_1(GNVP, 3)
    gnvp_tile(0, False, False)
    to_1(GNVP, 0)
    to_core(GNVP, 1, near_other)
    to_3(GRAD)
    to_2(GNVP)
    finish_queries(GRAD, oqg)
    to_3(GNVP)
    finish_entities(GRAD, oeg)
    finish_queries(GNVP, oqh)
    finish_entities(GNVP, oeh)
    for cp in started:
        cp.wait_send()


def store(a, b, c, d, to_a, to_b, to_c, to_d, sem):
    copies = [
        pltpu.make_async_copy(src, dst, sem.at[i])
        for i, (src, dst) in enumerate(((a, to_a), (b, to_b), (c, to_c), (d, to_d)))
    ]
    for cp in copies:
        cp.start()
    for cp in copies:
        cp.wait()


def per_device(ent_emb, ent_tan, qry_emb, qry_tan, tails):
    any_space = pl.BlockSpec(memory_space=pl.ANY)
    vmem = pl.BlockSpec(memory_space=pltpu.VMEM)
    dma = pltpu.SemaphoreType.DMA
    outs = (
        jax.ShapeDtypeStruct((SUB, D), F32),
        jax.ShapeDtypeStruct((SUB, D), F32),
        jax.ShapeDtypeStruct((32, D), F32),
        jax.ShapeDtypeStruct((32, D), F32),
    )
    results = pl.pallas_call(
        kernel,
        out_shape=outs,
        in_specs=[any_space] * 5,
        out_specs=[vmem] * 4,
        scratch_shapes=[
            pltpu.VMEM((4 * SUB, D), BF16),
            pltpu.VMEM((4 * SUB, D), BF16),
            pltpu.VMEM((4, PLANE, D), BF16),
            pltpu.VMEM((4, PLANE, D), BF16),
            pltpu.VMEM((4, 4 * PLANE), I32),
            pltpu.VMEM((4, 4, PLANE, 128), I32),
            pltpu.VMEM((2, 4, PLANE, 2 * SUB), F32),
            pltpu.VMEM((2, 4, PLANE, D), F32),
            pltpu.VMEM((2, 4 * SUB, D), F32),
            pltpu.VMEM((2, 2, SUB, D), F32),
            pltpu.VMEM((2, 2, 256, D), I16),
            pltpu.VMEM((2, 2, 256, D), I16),
            pltpu.VMEM((2, 2, 8, 128), F32),
            pltpu.VMEM((2, 2, 8, 128), F32),
            pltpu.VMEM((2, 4, PLANE, D), I16),
            pltpu.VMEM((2, 4, 8, 128), F32),
            pltpu.VMEM((2, 4, 128, D), I16),
            pltpu.VMEM((2, 4, 8, 128), F32),
            pltpu.VMEM((2, 4, 4, 32, D), I16),
            pltpu.VMEM((2, 4, 4, 8, 128), F32),
            pltpu.VMEM((2, 2, 128, D), F32),
            pltpu.VMEM((2, 8, 32, D), F32),
            pltpu.VMEM((2, 2, 32, D), F32),
            pltpu.VMEM((2, 2, 16, D), F32),
            dma((7,)),
            dma((2, A_N)),
            dma((2, A_N)),
            dma((2, 2, 2)),
            dma((2, 2, 2)),
            dma((2, 2)),
            dma((2, 2)),
            dma((2, 2)),
            dma((2, 2)),
            dma((2, 4)),
            dma((2, 4)),
            dma((2, 4)),
            dma((2, 4)),
            dma((2, 4, 4)),
            dma((2, 4, 4)),
            dma((2, 4, 4)),
            dma((2, 4, 4)),
            dma((2, 8)),
            dma((2, 8)),
            dma((2, 2)),
            dma((2, 2)),
        ],
        compiler_params=pltpu.CompilerParams(
            collective_id=0, has_side_effects=True, vmem_limit_bytes=VMEM_LIMIT
        ),
    )(ent_emb, ent_tan, qry_emb, qry_tan, tails.T)
    return pl.pallas_call(
        store,
        out_shape=outs,
        in_specs=[vmem] * 4,
        out_specs=[any_space] * 4,
        scratch_shapes=[dma((4,))],
        compiler_params=pltpu.CompilerParams(vmem_limit_bytes=8 * 2**20),
    )(*results)


def solution(mesh):
    return jax.shard_map(
        per_device,
        mesh=mesh,
        in_specs=(
            P("ent", None),
            P("ent", None),
            P(("qry", "ent"), None),
            P(("qry", "ent"), None),
            P("qry", None),
        ),
        out_specs=(
            P(("ent", "qry"), None),
            P(("ent", "qry"), None),
            P(("qry", "ent"), None),
            P(("qry", "ent"), None),
        ),
        check_vma=False,
    )
```

```python
import jax
import jax.numpy as jnp
from jax import lax
from jax.experimental import pallas as pl
from jax.experimental.pallas import tpu as pltpu
from jax.sharding import PartitionSpec as P

MESH = pl.DeviceIdType.MESH
F32 = jnp.float32
BF16 = jnp.bfloat16
I32 = jnp.int32
I16 = jnp.int16
D = 512
PLANE = 256
SUB = 512
NEAR_FIRST = (1, 3, 2)
VMEM_LIMIT = 50 * 2**20
GNVP, GRAD = 0, 1

A_X, A_Z, A_ZZ, A_XX, A_N = 0, 8, 16, 20, 36


def dot_nt(a, b):
    return lax.dot_general(a, b, (((1,), (1,)), ((), ())), preferred_element_type=F32)


def dot_tn(a, b):
    return lax.dot_general(a, b, (((0,), (0,)), ((), ())), preferred_element_type=F32)


def dot_nn(a, b):
    return lax.dot_general(a, b, (((1,), (0,)), ((), ())), preferred_element_type=F32)


def quantize(value, code_ref, scale_ref):
    top = jnp.max(jnp.abs(value), axis=(0, 1), keepdims=True)
    top = jnp.maximum(top, 1e-30)
    code_ref[...] = jnp.round(value * (32767.0 / top)).astype(I32).astype(I16)
    scale_ref[...] = jnp.broadcast_to(top * (1.0 / 32767.0), (8, 128))


def dequantize(code_ref, scale_ref):
    return code_ref[...].astype(I32).astype(F32) * scale_ref[0:1, 0:1]


def kernel(
    ent_hbm,
    ett_hbm,
    q_hbm,
    dq_hbm,
    tails_hbm,
    oeh,
    oeg,
    oqh,
    oqg,
    ent,
    ett,
    qp,
    dqp,
    tails,
    tb,
    w,
    qacc,
    eacc,
    drecv,
    csend,
    crecv,
    cssend,
    csrecv,
    bq,
    bqs,
    br0,
    br0s,
    br1,
    br1s,
    b2s,
    b2r,
    b3s,
    b3r,
    lsem,
    asend,
    arecv,
    dsend,
    drsem,
    cs_sem,
    cr_sem,
    css_sem,
    csr_sem,
    b0_ss,
    b0_rs,
    b0s_ss,
    b0s_rs,
    b1_ss,
    b1_rs,
    b1s_ss,
    b1s_rs,
    b2_ss,
    b2_rs,
    b3_ss,
    b3_rs,
):
    e_idx = lax.axis_index("ent")
    q_idx = lax.axis_index("qry")
    x, z, yl = e_idx // 8, (e_idx // 2) % 4, e_idx % 2
    yh, c = q_idx // 2, q_idx % 2

    def at(xx, zz, yy):
        return ((xx * 4 + zz) * 2 + yy, q_idx)

    def px(d, dy=0):
        return at((x + d) % 4, z, (yl + dy) % 2)

    def pz(d, dy=0):
        return at(x, (z + d) % 4, (yl + dy) % 2)

    py = at(x, z, 1 - yl)
    pcore = (e_idx, yh * 2 + 1 - c)
    phi = (e_idx, (1 - yh) * 2 + c)

    started = []

    def send(src, dst, ss, rs, peer):
        cp = pltpu.make_async_remote_copy(
            src_ref=src, dst_ref=dst, send_sem=ss, recv_sem=rs, device_id=peer, device_id_type=MESH
        )
        cp.start()
        started.append(cp)

    def arrived(dst, ss, rs):
        pltpu.make_async_remote_copy(
            src_ref=dst, dst_ref=dst, send_sem=ss, recv_sem=rs, device_id=py, device_id_type=MESH
        ).wait_recv()

    def rows(start, size, step):
        return pl.ds(pl.multiple_of(start, step), size)

    barrier = pltpu.get_barrier_semaphore()
    sides = [(d, dy) for d in (1, 2, 3) for dy in (0, 1)]
    for peer in [px(*s) for s in sides] + [pz(*s) for s in sides] + [py, pcore, phi]:
        pl.semaphore_signal(barrier, inc=1, device_id=peer, device_id_type=MESH)

    panel = (qp, dqp)
    own = (q_hbm, dq_hbm)
    my16 = [rows(h * 128 + x * 32 + yl * 16, 16, 16) for h in (0, 1)]

    local = []
    for a in (0, 1):
        for h in (0, 1):
            cp = pltpu.make_async_copy(
                own[a].at[pl.ds(h * 16, 16)], panel[a].at[z, my16[h]], lsem.at[a * 2 + h]
            )
            cp.start()
            local.append(cp)
    for i, (src, dst) in enumerate(((tails_hbm, tails), (ent_hbm, ent), (ett_hbm, ett))):
        cp = pltpu.make_async_copy(src, dst, lsem.at[4 + i])
        cp.start()
        local.append(cp)
    for cp in local[:4]:
        cp.wait()
    pl.semaphore_wait(barrier, 15)

    def slot(a, i):
        return asend.at[a, i], arecv.at[a, i]

    def first_sends(a):
        here = [panel[a].at[z, my16[h]] for h in (0, 1)]
        send(here[0], here[0], *slot(a, A_X + 1), py)
        send(here[1], here[1], *slot(a, A_Z + 1), py)
        for d in NEAR_FIRST:
            for dy in (0, 1):
                send(here[0], here[0], *slot(a, A_X + d * 2 + dy), px(d, dy))
                send(here[1], here[1], *slot(a, A_Z + d * 2 + dy), pz(d, dy))

    def first_arrived(a, d):
        for dy in (0, 1) if d else (1,):
            k = (yl + dy) % 2 * 16
            there = panel[a].at[z, rows(((x - d + 4) % 4) * 32 + k, 16, 16)]
            arrived(there, *slot(a, A_X + d * 2 + dy))
            there = panel[a].at[(z - d + 4) % 4, rows(128 + x * 32 + k, 16, 16)]
            arrived(there, *slot(a, A_Z + d * 2 + dy))

    def relays(a):
        for d in (0,) + NEAR_FIRST:
            first_arrived(a, d)
            if d == 0:
                relay_x(a, 0)
        for d in NEAR_FIRST:
            here = panel[a].at[z, pl.ds(0, 128)]
            send(here, here, *slot(a, A_ZZ + d), pz(d))
            relay_x(a, 4 - d)

    def relay_x(a, j):
        here = panel[a].at[(z + j) % 4, rows(128 + x * 32, 32, 32)]
        for e in NEAR_FIRST:
            send(here, here, *slot(a, A_XX + j * 4 + e), px(e))

    def plane_arrived(a, j):
        p = (z + j) % 4
        if j:
            arrived(panel[a].at[p, pl.ds(0, 128)], *slot(a, A_ZZ + 4 - j))
        for d in NEAR_FIRST:
            there = panel[a].at[p, rows(128 + ((x - d + 4) % 4) * 32, 32, 32)]
            arrived(there, *slot(a, A_XX + j * 4 + d))

    first_sends(0)
    first_sends(1)

    local[4].wait()

    def spread(m, _):
        for k in range(4):
            t = tails[pl.ds(k, 1), pl.ds(pl.multiple_of(m * 128, 128), 128)] - e_idx * (4 * SUB)
            t = jnp.broadcast_to(t, (128, 128)).T
            for i in range(8):
                to = rows(i % 2 * 128 + m // 2 * 32 + i // 2 % 2 * 16, 16, 16)
                tb[k, m % 2 * 2 + i // 4, to] = t[i * 16 : (i + 1) * 16]
        return 0

    lax.fori_loop(0, 8, spread, 0)
    relays(0)
    relays(1)
    local[5].wait()

    def add(ref, value, first):
        ref[...] = value if first else ref[...] + value

    def grad_tile(j, s, n, new, first):
        p = (z + j) % 4
        es = rows(s * SUB, n * SUB, SUB)
        q = qp[p]
        e = ent[es]
        score = dot_nt(q, e)
        lane = lax.broadcasted_iota(I32, (PLANE, 128), 1)
        label = []
        for b in range(n * SUB // 128):
            ids = lane + (s * SUB + b * 128)
            hit = tb[0, p] == ids
            for k in range(1, 4):
                hit = hit | (tb[k, p] == ids)
            label.append(jnp.where(hit, 1.0, 0.0).astype(F32))
        label = jnp.concatenate(label, axis=1)
        prob = 1.0 / (1.0 + jnp.exp(-score))
        slope = prob * (1.0 - prob)
        for i in range(n):
            w[p, s + i] = slope[:, i * SUB : (i + 1) * SUB]
        ugrad = (prob - label).astype(BF16)
        add(qacc.at[GRAD, p], dot_nn(ugrad, e), new)
        add(eacc.at[GRAD, es], dot_tn(ugrad, q), first)

    def gnvp_tile(j, s, n, new, first):
        p = (z + j) % 4
        es = rows(s * SUB, n * SUB, SUB)
        q = qp[p]
        e = ent[es]
        dscore = dot_nt(
            jnp.concatenate([dqp[p], q], axis=1), jnp.concatenate([e, ett[es]], axis=1)
        )
        slope = w[p, s] if n == 1 else jnp.concatenate([w[p, s + i] for i in range(n)], axis=1)
        uhess = (slope * dscore).astype(BF16)
        add(qacc.at[GNVP, p], dot_nn(uhess, e), new)
        add(eacc.at[GNVP, es], dot_tn(uhess, q), first)

    far_other = (1 - yh) * 2 + 1 - c
    far_same = (1 - yh) * 2 + c
    near_other = yh * 2 + 1 - c
    near_same = yh * 2 + c

    def to_core(k, i, s):
        for b in (0, 1):
            send(
                eacc.at[k, rows(s * SUB + b * 256, 256, 256)],
                drecv.at[k, i, pl.ds(b * 256, 256)],
                dsend.at[k, i, b],
                drsem.at[k, i, b],
                pcore,
            )

    def to_far(k):
        for b in (0, 1):
            here = drecv.at[k, 0, pl.ds(b * 256, 256)]
            arrived(here, dsend.at[k, 0, b], drsem.at[k, 0, b])
            value = eacc[k, rows(far_same * SUB + b * 256, 256, 256)] + here[...]
            quantize(value, csend.at[k, b], cssend.at[k, b])
            send(csend.at[k, b], crecv.at[k, b], cs_sem.at[k, b], cr_sem.at[k, b], phi)
            send(cssend.at[k, b], csrecv.at[k, b], css_sem.at[k, b], csr_sem.at[k, b], phi)

    def finish_entities(k, out):
        for b in (0, 1):
            here = drecv.at[k, 1, pl.ds(b * 256, 256)]
            arrived(here, dsend.at[k, 1, b], drsem.at[k, 1, b])
            arrived(csrecv.at[k, b], css_sem.at[k, b], csr_sem.at[k, b])
            arrived(crecv.at[k, b], cs_sem.at[k, b], cr_sem.at[k, b])
            out[pl.ds(b * 256, 256)] = (
                eacc[k, rows(near_same * SUB + b * 256, 256, 256)]
                + here[...]
                + dequantize(crecv.at[k, b], csrecv.at[k, b])
            )

    def to_1(k, j):
        p = (z + j) % 4
        quantize(qacc[k, p], bq.at[k, j], bqs.at[k, j])
        if j:
            send(bqs.at[k, j], br0s.at[k, j], b0s_ss.at[k, j], b0s_rs.at[k, j], pz(j))
            here = bq.at[k, j, pl.ds(0, 128)]
            send(here, br0.at[k, j], b0_ss.at[k, j], b0_rs.at[k, j], pz(j))
        for d in NEAR_FIRST:
            send(bqs.at[k, j], br1s.at[k, j, d], b1s_ss.at[k, j, d], b1s_rs.at[k, j, d], px(d))
            here = bq.at[k, j, rows(128 + ((x + d) % 4) * 32, 32, 32)]
            send(here, br1.at[k, j, d], b1_ss.at[k, j, d], b1_rs.at[k, j, d], px(d))

    def to_2(k):
        total = qacc[k, z, pl.ds(0, 128)]
        for j in NEAR_FIRST:
            arrived(br0s.at[k, j], b0s_ss.at[k, j], b0s_rs.at[k, j])
            arrived(br0.at[k, j], b0_ss.at[k, j], b0_rs.at[k, j])
            total = total + dequantize(br0.at[k, j], br0s.at[k, j])
        b2s[k, 0] = total
        for d in NEAR_FIRST:
            here = b2s.at[k, 0, rows(((x + d) % 4) * 32, 32, 32)]
            send(here, b2r.at[k, d], b2_ss.at[k, d], b2_rs.at[k, d], px(d))
        for j in (3, 1, 2, 0):
            total = qacc[k, (z + j) % 4, rows(128 + x * 32, 32, 32)]
            for d in NEAR_FIRST:
                arrived(br1s.at[k, j, d], b1s_ss.at[k, j, d], b1s_rs.at[k, j, d])
                arrived(br1.at[k, j, d], b1_ss.at[k, j, d], b1_rs.at[k, j, d])
                total = total + dequantize(br1.at[k, j, d], br1s.at[k, j, d])
            b2s[k, 1, pl.ds(j * 32, 32)] = total
            if j:
                here = b2s.at[k, 1, pl.ds(j * 32, 32)]
                send(here, b2r.at[k, 4 + j], b2_ss.at[k, 4 + j], b2_rs.at[k, 4 + j], pz(j))

    def to_3(k):
        for h in (0, 1):
            total = b2s[k, 0, rows(x * 32, 32, 32)] if h == 0 else b2s[k, 1, pl.ds(0, 32)]
            for d in NEAR_FIRST:
                i = h * 4 + d
                arrived(b2r.at[k, i], b2_ss.at[k, i], b2_rs.at[k, i])
                total = total + b2r[k, i]
            b3s[k, h] = total
            here = b3s.at[k, h, rows((1 - yl) * 16, 16, 16)]
            send(here, b3r.at[k, h], b3_ss.at[k, h], b3_rs.at[k, h], py)

    def finish_queries(k, out):
        for h in (0, 1):
            arrived(b3r.at[k, h], b3_ss.at[k, h], b3_rs.at[k, h])
            out[pl.ds(h * 16, 16)] = b3s[k, h, rows(yl * 16, 16, 16)] + b3r[k, h]

    far, near = (1 - yh) * 2, yh * 2
    for j in (0, 3, 1):
        plane_arrived(0, j)
        grad_tile(j, far, 2, True, j == 0)
    plane_arrived(0, 2)
    grad_tile(2, far_other, 1, True, False)
    to_core(GRAD, 0, far_other)
    grad_tile(2, far_same, 1, False, False)
    local[6].wait()
    for j in (3, 1, 2):
        grad_tile(j, near, 2, False, j == 3)
        if j == 3:
            to_far(GRAD)
        to_1(GRAD, j)
        plane_arrived(1, j)
        gnvp_tile(j, far, 2, True, j == 3)
        gnvp_tile(j, near, 2, False, j == 3)
        to_1(GNVP, j)
    plane_arrived(1, 0)
    gnvp_tile(0, far_other, 1, True, False)
    to_core(GNVP, 0, far_other)
    gnvp_tile(0, far_same, 1, False, False)
    grad_tile(0, near, 2, False, False)
    to_core(GRAD, 1, near_other)
    to_1(GRAD, 0)
    to_far(GNVP)
    gnvp_tile(0, near, 2, False, False)
    to_core(GNVP, 1, near_other)
    to_1(GNVP, 0)
    to_2(GRAD)
    to_2(GNVP)
    to_3(GRAD)
    to_3(GNVP)
    finish_entities(GRAD, oeg)
    finish_queries(GRAD, oqg)
    finish_queries(GNVP, oqh)
    finish_entities(GNVP, oeh)
    for cp in started:
        cp.wait_send()


def store(a, b, c, d, to_a, to_b, to_c, to_d, sem):
    copies = [
        pltpu.make_async_copy(src, dst, sem.at[i])
        for i, (src, dst) in enumerate(((a, to_a), (b, to_b), (c, to_c), (d, to_d)))
    ]
    for cp in copies:
        cp.start()
    for cp in copies:
        cp.wait()


def per_device(ent_emb, ent_tan, qry_emb, qry_tan, tails):
    any_space = pl.BlockSpec(memory_space=pl.ANY)
    vmem = pl.BlockSpec(memory_space=pltpu.VMEM)
    dma = pltpu.SemaphoreType.DMA
    outs = (
        jax.ShapeDtypeStruct((SUB, D), F32),
        jax.ShapeDtypeStruct((SUB, D), F32),
        jax.ShapeDtypeStruct((32, D), F32),
        jax.ShapeDtypeStruct((32, D), F32),
    )
    results = pl.pallas_call(
        kernel,
        out_shape=outs,
        in_specs=[pl.BlockSpec(memory_space=pltpu.HBM)] * 5,
        out_specs=[vmem] * 4,
        scratch_shapes=[
            pltpu.VMEM((4 * SUB, D), BF16),
            pltpu.VMEM((4 * SUB, D), BF16),
            pltpu.VMEM((4, PLANE, D), BF16),
            pltpu.VMEM((4, PLANE, D), BF16),
            pltpu.VMEM((4, 4 * PLANE), I32),
            pltpu.VMEM((4, 4, PLANE, 128), I32),
            pltpu.VMEM((4, 4, PLANE, SUB), F32),
            pltpu.VMEM((2, 4, PLANE, D), F32),
            pltpu.VMEM((2, 4 * SUB, D), F32),
            pltpu.VMEM((2, 2, SUB, D), F32),
            pltpu.VMEM((2, 2, 256, D), I16),
            pltpu.VMEM((2, 2, 256, D), I16),
            pltpu.VMEM((2, 2, 8, 128), F32),
            pltpu.VMEM((2, 2, 8, 128), F32),
            pltpu.VMEM((2, 4, PLANE, D), I16),
            pltpu.VMEM((2, 4, 8, 128), F32),
            pltpu.VMEM((2, 4, 128, D), I16),
            pltpu.VMEM((2, 4, 8, 128), F32),
            pltpu.VMEM((2, 4, 4, 32, D), I16),
            pltpu.VMEM((2, 4, 4, 8, 128), F32),
            pltpu.VMEM((2, 2, 128, D), F32),
            pltpu.VMEM((2, 8, 32, D), F32),
            pltpu.VMEM((2, 2, 32, D), F32),
            pltpu.VMEM((2, 2, 16, D), F32),
            dma((7,)),
            dma((2, A_N)),
            dma((2, A_N)),
            dma((2, 2, 2)),
            dma((2, 2, 2)),
            dma((2, 2)),
            dma((2, 2)),
            dma((2, 2)),
            dma((2, 2)),
            dma((2, 4)),
            dma((2, 4)),
            dma((2, 4)),
            dma((2, 4)),
            dma((2, 4, 4)),
            dma((2, 4, 4)),
            dma((2, 4, 4)),
            dma((2, 4, 4)),
            dma((2, 8)),
            dma((2, 8)),
            dma((2, 2)),
            dma((2, 2)),
        ],
        compiler_params=pltpu.CompilerParams(
            collective_id=0, has_side_effects=True, vmem_limit_bytes=VMEM_LIMIT
        ),
    )(ent_emb, ent_tan, qry_emb, qry_tan, tails.T)
    return pl.pallas_call(
        store,
        out_shape=outs,
        in_specs=[vmem] * 4,
        out_specs=[any_space] * 4,
        scratch_shapes=[dma((4,))],
        compiler_params=pltpu.CompilerParams(vmem_limit_bytes=8 * 2**20),
    )(*results)


def solution(mesh):
    return jax.shard_map(
        per_device,
        mesh=mesh,
        in_specs=(
            P("ent", None),
            P("ent", None),
            P(("qry", "ent"), None),
            P(("qry", "ent"), None),
            P("qry", None),
        ),
        out_specs=(
            P(("ent", "qry"), None),
            P(("ent", "qry"), None),
            P(("qry", "ent"), None),
            P(("qry", "ent"), None),
        ),
        check_vma=False,
    )
```

```python
import jax
import jax.numpy as jnp
from jax import lax
from jax.experimental import pallas as pl
from jax.experimental.pallas import tpu as pltpu
from jax.sharding import PartitionSpec as P

MESH = pl.DeviceIdType.MESH
F32 = jnp.float32
BF16 = jnp.bfloat16
I32 = jnp.int32
I16 = jnp.int16
D = 512
PLANE = 256
SUB = 512
NEAR_FIRST = (1, 3, 2)
VMEM_LIMIT = 50 * 2**20
GNVP, GRAD = 0, 1

A_X, A_Z, A_ZZ, A_XX, A_N = 0, 8, 16, 32, 48


def dot_nt(a, b):
    return lax.dot_general(a, b, (((1,), (1,)), ((), ())), preferred_element_type=F32)


def dot_tn(a, b):
    return lax.dot_general(a, b, (((0,), (0,)), ((), ())), preferred_element_type=F32)


def dot_nn(a, b):
    return lax.dot_general(a, b, (((1,), (0,)), ((), ())), preferred_element_type=F32)


def quantize(value, code_ref, scale_ref):
    top = jnp.max(jnp.abs(value), axis=(0, 1), keepdims=True)
    top = jnp.maximum(top, 1e-30)
    code_ref[...] = jnp.round(value * (32767.0 / top)).astype(I32).astype(I16)
    scale_ref[...] = jnp.broadcast_to(top * (1.0 / 32767.0), (8, 128))


def dequantize(code_ref, scale_ref):
    return code_ref[...].astype(I32).astype(F32) * scale_ref[0:1, 0:1]


def kernel(
    ent_hbm,
    ett_hbm,
    q_hbm,
    dq_hbm,
    tails_hbm,
    oeh,
    oeg,
    oqh,
    oqg,
    ent,
    ett,
    qp,
    dqp,
    tails,
    tb,
    w,
    qacc,
    eacc,
    drecv,
    csend,
    crecv,
    cssend,
    csrecv,
    bq,
    bqs,
    br0,
    br0s,
    br1,
    br1s,
    b2s,
    b2r,
    b3s,
    b3r,
    lsem,
    asend,
    arecv,
    dsend,
    drsem,
    cs_sem,
    cr_sem,
    css_sem,
    csr_sem,
    b0_ss,
    b0_rs,
    b0s_ss,
    b0s_rs,
    b1_ss,
    b1_rs,
    b1s_ss,
    b1s_rs,
    b2_ss,
    b2_rs,
    b3_ss,
    b3_rs,
):
    e_idx = lax.axis_index("ent")
    q_idx = lax.axis_index("qry")
    x, z, yl = e_idx // 8, (e_idx // 2) % 4, e_idx % 2
    yh, c = q_idx // 2, q_idx % 2

    def at(xx, zz, yy):
        return ((xx * 4 + zz) * 2 + yy, q_idx)

    def px(d, dy=0):
        return at((x + d) % 4, z, (yl + dy) % 2)

    def pz(d, dy=0):
        return at(x, (z + d) % 4, (yl + dy) % 2)

    py = at(x, z, 1 - yl)
    pcore = (e_idx, yh * 2 + 1 - c)
    phi = (e_idx, (1 - yh) * 2 + c)

    started = []

    def send(src, dst, ss, rs, peer):
        cp = pltpu.make_async_remote_copy(
            src_ref=src, dst_ref=dst, send_sem=ss, recv_sem=rs, device_id=peer, device_id_type=MESH
        )
        cp.start()
        started.append(cp)

    def arrived(dst, ss, rs):
        pltpu.make_async_remote_copy(
            src_ref=dst, dst_ref=dst, send_sem=ss, recv_sem=rs, device_id=py, device_id_type=MESH
        ).wait_recv()

    def rows(start, size, step):
        return pl.ds(pl.multiple_of(start, step), size)

    barrier = pltpu.get_barrier_semaphore()
    sides = [(d, dy) for d in (1, 2, 3) for dy in (0, 1)]
    for peer in [px(*s) for s in sides] + [pz(*s) for s in sides] + [py, pcore, phi]:
        pl.semaphore_signal(barrier, inc=1, device_id=peer, device_id_type=MESH)

    panel = (qp, dqp)
    own = (q_hbm, dq_hbm)
    my16 = [rows(h * 128 + x * 32 + yl * 16, 16, 16) for h in (0, 1)]

    local = []
    for a in (0, 1):
        for h in (0, 1):
            cp = pltpu.make_async_copy(
                own[a].at[pl.ds(h * 16, 16)], panel[a].at[z, my16[h]], lsem.at[a * 2 + h]
            )
            cp.start()
            local.append(cp)
    for i, (src, dst) in enumerate(((tails_hbm, tails), (ent_hbm, ent), (ett_hbm, ett))):
        cp = pltpu.make_async_copy(src, dst, lsem.at[4 + i])
        cp.start()
        local.append(cp)
    for cp in local[:4]:
        cp.wait()
    pl.semaphore_wait(barrier, 15)

    def slot(a, i):
        return asend.at[a, i], arecv.at[a, i]

    def first_sends(a):
        here = [panel[a].at[z, my16[h]] for h in (0, 1)]
        send(here[0], here[0], *slot(a, A_X + 1), py)
        send(here[1], here[1], *slot(a, A_Z + 1), py)
        for d in NEAR_FIRST:
            for dy in (0, 1):
                send(here[0], here[0], *slot(a, A_X + d * 2 + dy), px(d, dy))
                send(here[1], here[1], *slot(a, A_Z + d * 2 + dy), pz(d, dy))

    def first_arrived(a, d):
        for dy in (0, 1) if d else (1,):
            k = (yl + dy) % 2 * 16
            there = panel[a].at[z, rows(((x - d + 4) % 4) * 32 + k, 16, 16)]
            arrived(there, *slot(a, A_X + d * 2 + dy))
            there = panel[a].at[(z - d + 4) % 4, rows(128 + x * 32 + k, 16, 16)]
            arrived(there, *slot(a, A_Z + d * 2 + dy))

    def relays(a):
        for d in (0,) + NEAR_FIRST:
            first_arrived(a, d)
            j = (4 - d) % 4
            here = panel[a].at[z, rows(((x + j) % 4) * 32, 32, 32)]
            for e in NEAR_FIRST:
                send(here, here, *slot(a, A_ZZ + j * 4 + e), pz(e))
            here = panel[a].at[(z + j) % 4, rows(128 + x * 32, 32, 32)]
            for e in NEAR_FIRST:
                send(here, here, *slot(a, A_XX + j * 4 + e), px(e))

    def plane_arrived(a, j):
        p = (z + j) % 4
        if j:
            for i in range(4):
                there = panel[a].at[p, rows(((x + i) % 4) * 32, 32, 32)]
                arrived(there, *slot(a, A_ZZ + i * 4 + (4 - j)))
        for d in NEAR_FIRST:
            there = panel[a].at[p, rows(128 + ((x - d + 4) % 4) * 32, 32, 32)]
            arrived(there, *slot(a, A_XX + j * 4 + d))

    first_sends(0)

    local[4].wait()

    def spread(m, _):
        for k in range(4):
            t = tails[pl.ds(k, 1), pl.ds(pl.multiple_of(m * 128, 128), 128)] - e_idx * (4 * SUB)
            t = jnp.broadcast_to(t, (128, 128)).T
            for i in range(8):
                to = rows(i % 2 * 128 + m // 2 * 32 + i // 2 % 2 * 16, 16, 16)
                tb[k, m % 2 * 2 + i // 4, to] = t[i * 16 : (i + 1) * 16]
        return 0

    lax.fori_loop(0, 8, spread, 0)
    relays(0)
    first_sends(1)
    local[5].wait()

    def add(ref, value, first):
        ref[...] = value if first else ref[...] + value

    def grad_tile(j, far, first):
        p = (z + j) % 4
        half = 1 - yh if far else yh
        es = rows(half * 2 * SUB, 2 * SUB, 2 * SUB)
        q = qp[p]
        e = ent[es]
        score = dot_nt(q, e)
        lane = lax.broadcasted_iota(I32, (PLANE, 128), 1)
        label = []
        for b in range(2 * SUB // 128):
            ids = lane + (half * 2 * SUB + b * 128)
            hit = tb[0, p] == ids
            for k in range(1, 4):
                hit = hit | (tb[k, p] == ids)
            label.append(jnp.where(hit, 1.0, 0.0).astype(F32))
        label = jnp.concatenate(label, axis=1)
        prob = 1.0 / (1.0 + jnp.exp(-score))
        w[half, p] = prob * (1.0 - prob)
        ugrad = (prob - label).astype(BF16)
        add(qacc.at[GRAD, p], dot_nn(ugrad, e), far)
        add(eacc.at[GRAD, es], dot_tn(ugrad, q), first)

    def gnvp_tile(j, far, first):
        p = (z + j) % 4
        half = 1 - yh if far else yh
        es = rows(half * 2 * SUB, 2 * SUB, 2 * SUB)
        q = qp[p]
        e = ent[es]
        dscore = dot_nt(
            jnp.concatenate([dqp[p], q], axis=1), jnp.concatenate([e, ett[es]], axis=1)
        )
        uhess = (w[half, p] * dscore).astype(BF16)
        add(qacc.at[GNVP, p], dot_nn(uhess, e), far)
        add(eacc.at[GNVP, es], dot_tn(uhess, q), first)

    far_other = (1 - yh) * 2 + 1 - c
    far_same = (1 - yh) * 2 + c
    near_other = yh * 2 + 1 - c
    near_same = yh * 2 + c

    def to_core(k, i, s):
        for b in (0, 1):
            send(
                eacc.at[k, rows(s * SUB + b * 256, 256, 256)],
                drecv.at[k, i, pl.ds(b * 256, 256)],
                dsend.at[k, i, b],
                drsem.at[k, i, b],
                pcore,
            )

    def to_far(k):
        for b in (0, 1):
            here = drecv.at[k, 0, pl.ds(b * 256, 256)]
            arrived(here, dsend.at[k, 0, b], drsem.at[k, 0, b])
            value = eacc[k, rows(far_same * SUB + b * 256, 256, 256)] + here[...]
            quantize(value, csend.at[k, b], cssend.at[k, b])
            send(csend.at[k, b], crecv.at[k, b], cs_sem.at[k, b], cr_sem.at[k, b], phi)
            send(cssend.at[k, b], csrecv.at[k, b], css_sem.at[k, b], csr_sem.at[k, b], phi)

    def finish_entities(k, out):
        for b in (0, 1):
            here = drecv.at[k, 1, pl.ds(b * 256, 256)]
            arrived(here, dsend.at[k, 1, b], drsem.at[k, 1, b])
            arrived(csrecv.at[k, b], css_sem.at[k, b], csr_sem.at[k, b])
            arrived(crecv.at[k, b], cs_sem.at[k, b], cr_sem.at[k, b])
            out[pl.ds(b * 256, 256)] = (
                eacc[k, rows(near_same * SUB + b * 256, 256, 256)]
                + here[...]
                + dequantize(crecv.at[k, b], csrecv.at[k, b])
            )

    def to_1(k, j):
        p = (z + j) % 4
        quantize(qacc[k, p], bq.at[k, j], bqs.at[k, j])
        if j:
            send(bqs.at[k, j], br0s.at[k, j], b0s_ss.at[k, j], b0s_rs.at[k, j], pz(j))
            here = bq.at[k, j, pl.ds(0, 128)]
            send(here, br0.at[k, j], b0_ss.at[k, j], b0_rs.at[k, j], pz(j))
        for d in NEAR_FIRST:
            send(bqs.at[k, j], br1s.at[k, j, d], b1s_ss.at[k, j, d], b1s_rs.at[k, j, d], px(d))
            here = bq.at[k, j, rows(128 + ((x + d) % 4) * 32, 32, 32)]
            send(here, br1.at[k, j, d], b1_ss.at[k, j, d], b1_rs.at[k, j, d], px(d))

    def to_2(k):
        total = qacc[k, z, pl.ds(0, 128)]
        for j in NEAR_FIRST:
            arrived(br0s.at[k, j], b0s_ss.at[k, j], b0s_rs.at[k, j])
            arrived(br0.at[k, j], b0_ss.at[k, j], b0_rs.at[k, j])
            total = total + dequantize(br0.at[k, j], br0s.at[k, j])
        b2s[k, 0] = total
        for d in NEAR_FIRST:
            here = b2s.at[k, 0, rows(((x + d) % 4) * 32, 32, 32)]
            send(here, b2r.at[k, d], b2_ss.at[k, d], b2_rs.at[k, d], px(d))
        for j in (2, 1, 3, 0):
            total = qacc[k, (z + j) % 4, rows(128 + x * 32, 32, 32)]
            for d in NEAR_FIRST:
                arrived(br1s.at[k, j, d], b1s_ss.at[k, j, d], b1s_rs.at[k, j, d])
                arrived(br1.at[k, j, d], b1_ss.at[k, j, d], b1_rs.at[k, j, d])
                total = total + dequantize(br1.at[k, j, d], br1s.at[k, j, d])
            b2s[k, 1, pl.ds(j * 32, 32)] = total
            if j:
                here = b2s.at[k, 1, pl.ds(j * 32, 32)]
                send(here, b2r.at[k, 4 + j], b2_ss.at[k, 4 + j], b2_rs.at[k, 4 + j], pz(j))

    def to_3(k):
        for h in (0, 1):
            total = b2s[k, 0, rows(x * 32, 32, 32)] if h == 0 else b2s[k, 1, pl.ds(0, 32)]
            for d in NEAR_FIRST:
                i = h * 4 + d
                arrived(b2r.at[k, i], b2_ss.at[k, i], b2_rs.at[k, i])
                total = total + b2r[k, i]
            b3s[k, h] = total
            here = b3s.at[k, h, rows((1 - yl) * 16, 16, 16)]
            send(here, b3r.at[k, h], b3_ss.at[k, h], b3_rs.at[k, h], py)

    def finish_queries(k, out):
        for h in (0, 1):
            arrived(b3r.at[k, h], b3_ss.at[k, h], b3_rs.at[k, h])
            out[pl.ds(h * 16, 16)] = b3s[k, h, rows(yl * 16, 16, 16)] + b3r[k, h]

    for j in (0,) + NEAR_FIRST:
        plane_arrived(0, j)
        grad_tile(j, True, j == 0)
    to_core(GRAD, 0, far_other)
    relays(1)
    grad_tile(2, False, True)
    to_far(GRAD)
    to_1(GRAD, 2)
    grad_tile(1, False, False)
    to_1(GRAD, 1)
    grad_tile(3, False, False)
    to_1(GRAD, 3)
    grad_tile(0, False, False)
    to_1(GRAD, 0)
    to_core(GRAD, 1, near_other)
    local[6].wait()
    for j in (0,) + NEAR_FIRST:
        plane_arrived(1, j)
        gnvp_tile(j, True, j == 0)
    to_core(GNVP, 0, far_other)
    gnvp_tile(2, False, True)
    to_1(GNVP, 2)
    gnvp_tile(1, False, False)
    to_far(GNVP)
    to_1(GNVP, 1)
    to_2(GRAD)
    gnvp_tile(3, False, False)
    to_1(GNVP, 3)
    gnvp_tile(0, False, False)
    to_1(GNVP, 0)
    to_core(GNVP, 1, near_other)
    to_3(GRAD)
    to_2(GNVP)
    finish_queries(GRAD, oqg)
    to_3(GNVP)
    finish_entities(GRAD, oeg)
    finish_queries(GNVP, oqh)
    finish_entities(GNVP, oeh)
    for cp in started:
        cp.wait_send()


def store(a, b, c, d, to_a, to_b, to_c, to_d, sem):
    copies = [
        pltpu.make_async_copy(src, dst, sem.at[i])
        for i, (src, dst) in enumerate(((a, to_a), (b, to_b), (c, to_c), (d, to_d)))
    ]
    for cp in copies:
        cp.start()
    for cp in copies:
        cp.wait()


def per_device(ent_emb, ent_tan, qry_emb, qry_tan, tails):
    any_space = pl.BlockSpec(memory_space=pl.ANY)
    vmem = pl.BlockSpec(memory_space=pltpu.VMEM)
    dma = pltpu.SemaphoreType.DMA
    outs = (
        jax.ShapeDtypeStruct((SUB, D), F32),
        jax.ShapeDtypeStruct((SUB, D), F32),
        jax.ShapeDtypeStruct((32, D), F32),
        jax.ShapeDtypeStruct((32, D), F32),
    )
    results = pl.pallas_call(
        kernel,
        out_shape=outs,
        in_specs=[pl.BlockSpec(memory_space=pltpu.HBM)] * 5,
        out_specs=[vmem] * 4,
        scratch_shapes=[
            pltpu.VMEM((4 * SUB, D), BF16),
            pltpu.VMEM((4 * SUB, D), BF16),
            pltpu.VMEM((4, PLANE, D), BF16),
            pltpu.VMEM((4, PLANE, D), BF16),
            pltpu.VMEM((4, 4 * PLANE), I32),
            pltpu.VMEM((4, 4, PLANE, 128), I32),
            pltpu.VMEM((2, 4, PLANE, 2 * SUB), F32),
            pltpu.VMEM((2, 4, PLANE, D), F32),
            pltpu.VMEM((2, 4 * SUB, D), F32),
            pltpu.VMEM((2, 2, SUB, D), F32),
            pltpu.VMEM((2, 2, 256, D), I16),
            pltpu.VMEM((2, 2, 256, D), I16),
            pltpu.VMEM((2, 2, 8, 128), F32),
            pltpu.VMEM((2, 2, 8, 128), F32),
            pltpu.VMEM((2, 4, PLANE, D), I16),
            pltpu.VMEM((2, 4, 8, 128), F32),
            pltpu.VMEM((2, 4, 128, D), I16),
            pltpu.VMEM((2, 4, 8, 128), F32),
            pltpu.VMEM((2, 4, 4, 32, D), I16),
            pltpu.VMEM((2, 4, 4, 8, 128), F32),
            pltpu.VMEM((2, 2, 128, D), F32),
            pltpu.VMEM((2, 8, 32, D), F32),
            pltpu.VMEM((2, 2, 32, D), F32),
            pltpu.VMEM((2, 2, 16, D), F32),
            dma((7,)),
            dma((2, A_N)),
            dma((2, A_N)),
            dma((2, 2, 2)),
            dma((2, 2, 2)),
            dma((2, 2)),
            dma((2, 2)),
            dma((2, 2)),
            dma((2, 2)),
            dma((2, 4)),
            dma((2, 4)),
            dma((2, 4)),
            dma((2, 4)),
            dma((2, 4, 4)),
            dma((2, 4, 4)),
            dma((2, 4, 4)),
            dma((2, 4, 4)),
            dma((2, 8)),
            dma((2, 8)),
            dma((2, 2)),
            dma((2, 2)),
        ],
        compiler_params=pltpu.CompilerParams(
            collective_id=0, has_side_effects=True, vmem_limit_bytes=VMEM_LIMIT
        ),
    )(*[pltpu.with_memory_space_constraint(a, pltpu.HBM) for a in (ent_emb, ent_tan, qry_emb, qry_tan, tails.T)])
    return pl.pallas_call(
        store,
        out_shape=outs,
        in_specs=[vmem] * 4,
        out_specs=[any_space] * 4,
        scratch_shapes=[dma((4,))],
        compiler_params=pltpu.CompilerParams(vmem_limit_bytes=8 * 2**20),
    )(*results)


def solution(mesh):
    return jax.shard_map(
        per_device,
        mesh=mesh,
        in_specs=(
            P("ent", None),
            P("ent", None),
            P(("qry", "ent"), None),
            P(("qry", "ent"), None),
            P("qry", None),
        ),
        out_specs=(
            P(("ent", "qry"), None),
            P(("ent", "qry"), None),
            P(("qry", "ent"), None),
            P(("qry", "ent"), None),
        ),
        check_vma=False,
    )
```

```python
import jax
import jax.numpy as jnp
from jax import lax
from jax.experimental import pallas as pl
from jax.experimental.pallas import tpu as pltpu
from jax.sharding import PartitionSpec as P

MESH = pl.DeviceIdType.MESH
F32 = jnp.float32
BF16 = jnp.bfloat16
I32 = jnp.int32
I16 = jnp.int16
D = 512
PLANE = 256
SUB = 512
NEAR_FIRST = (1, 3, 2)
VMEM_LIMIT = 50 * 2**20
GNVP, GRAD = 0, 1

A_X, A_Z, A_ZZ, A_XX, A_N = 0, 8, 16, 32, 48


def dot_nt(a, b):
    return lax.dot_general(a, b, (((1,), (1,)), ((), ())), preferred_element_type=F32)


def dot_tn(a, b):
    return lax.dot_general(a, b, (((0,), (0,)), ((), ())), preferred_element_type=F32)


def dot_nn(a, b):
    return lax.dot_general(a, b, (((1,), (0,)), ((), ())), preferred_element_type=F32)


def quantize(value, code_ref, scale_ref):
    top = jnp.max(jnp.abs(value), axis=(0, 1), keepdims=True)
    top = jnp.maximum(top, 1e-30)
    code_ref[...] = jnp.round(value * (32767.0 / top)).astype(I32).astype(I16)
    scale_ref[...] = jnp.broadcast_to(top * (1.0 / 32767.0), (8, 128))


def dequantize(code_ref, scale_ref):
    return code_ref[...].astype(I32).astype(F32) * scale_ref[0:1, 0:1]


def kernel(
    ent_hbm,
    ett_hbm,
    q_hbm,
    dq_hbm,
    tails_hbm,
    oeh,
    oeg,
    oqh,
    oqg,
    ent,
    ett,
    qp,
    dqp,
    tails,
    tb,
    w,
    qacc,
    eacc,
    drecv,
    csend,
    crecv,
    cssend,
    csrecv,
    bq,
    bqs,
    br0,
    br0s,
    br1,
    br1s,
    b2s,
    b2q,
    b2qs,
    b2r,
    b2rs,
    b3s,
    b3r,
    lsem,
    asend,
    arecv,
    dsend,
    drsem,
    cs_sem,
    cr_sem,
    css_sem,
    csr_sem,
    b0_ss,
    b0_rs,
    b0s_ss,
    b0s_rs,
    b1_ss,
    b1_rs,
    b1s_ss,
    b1s_rs,
    b2_ss,
    b2_rs,
    b2s_ss,
    b2s_rs,
    b3_ss,
    b3_rs,
):
    e_idx = lax.axis_index("ent")
    q_idx = lax.axis_index("qry")
    x, z, yl = e_idx // 8, (e_idx // 2) % 4, e_idx % 2
    yh, c = q_idx // 2, q_idx % 2

    def at(xx, zz, yy):
        return ((xx * 4 + zz) * 2 + yy, q_idx)

    def px(d, dy=0):
        return at((x + d) % 4, z, (yl + dy) % 2)

    def pz(d, dy=0):
        return at(x, (z + d) % 4, (yl + dy) % 2)

    py = at(x, z, 1 - yl)
    pcore = (e_idx, yh * 2 + 1 - c)
    phi = (e_idx, (1 - yh) * 2 + c)

    started = []

    def send(src, dst, ss, rs, peer):
        cp = pltpu.make_async_remote_copy(
            src_ref=src, dst_ref=dst, send_sem=ss, recv_sem=rs, device_id=peer, device_id_type=MESH
        )
        cp.start()
        started.append(cp)

    def arrived(dst, ss, rs):
        pltpu.make_async_remote_copy(
            src_ref=dst, dst_ref=dst, send_sem=ss, recv_sem=rs, device_id=py, device_id_type=MESH
        ).wait_recv()

    def rows(start, size, step):
        return pl.ds(pl.multiple_of(start, step), size)

    barrier = pltpu.get_barrier_semaphore()
    sides = [(d, dy) for d in (1, 2, 3) for dy in (0, 1)]
    for peer in [px(*s) for s in sides] + [pz(*s) for s in sides] + [py, pcore, phi]:
        pl.semaphore_signal(barrier, inc=1, device_id=peer, device_id_type=MESH)

    panel = (qp, dqp)
    own = (q_hbm, dq_hbm)
    my16 = [rows(h * 128 + x * 32 + yl * 16, 16, 16) for h in (0, 1)]

    local = []
    for a in (0, 1):
        for h in (0, 1):
            cp = pltpu.make_async_copy(
                own[a].at[pl.ds(h * 16, 16)], panel[a].at[z, my16[h]], lsem.at[a * 2 + h]
            )
            cp.start()
            local.append(cp)
    for i, (src, dst) in enumerate(((tails_hbm, tails), (ent_hbm, ent), (ett_hbm, ett))):
        cp = pltpu.make_async_copy(src, dst, lsem.at[4 + i])
        cp.start()
        local.append(cp)
    for cp in local[:4]:
        cp.wait()
    pl.semaphore_wait(barrier, 15)

    def slot(a, i):
        return asend.at[a, i], arecv.at[a, i]

    def first_sends(a):
        here = [panel[a].at[z, my16[h]] for h in (0, 1)]
        send(here[0], here[0], *slot(a, A_X + 1), py)
        send(here[1], here[1], *slot(a, A_Z + 1), py)
        for d in NEAR_FIRST:
            for dy in (0, 1):
                send(here[0], here[0], *slot(a, A_X + d * 2 + dy), px(d, dy))
                send(here[1], here[1], *slot(a, A_Z + d * 2 + dy), pz(d, dy))

    def first_arrived(a, d):
        for dy in (0, 1) if d else (1,):
            k = (yl + dy) % 2 * 16
            there = panel[a].at[z, rows(((x - d + 4) % 4) * 32 + k, 16, 16)]
            arrived(there, *slot(a, A_X + d * 2 + dy))
            there = panel[a].at[(z - d + 4) % 4, rows(128 + x * 32 + k, 16, 16)]
            arrived(there, *slot(a, A_Z + d * 2 + dy))

    def relays(a):
        for d in (0,) + NEAR_FIRST:
            first_arrived(a, d)
            j = (4 - d) % 4
            here = panel[a].at[z, rows(((x + j) % 4) * 32, 32, 32)]
            for e in NEAR_FIRST:
                send(here, here, *slot(a, A_ZZ + j * 4 + e), pz(e))
            here = panel[a].at[(z + j) % 4, rows(128 + x * 32, 32, 32)]
            for e in NEAR_FIRST:
                send(here, here, *slot(a, A_XX + j * 4 + e), px(e))

    def plane_arrived(a, j):
        p = (z + j) % 4
        if j:
            for i in range(4):
                there = panel[a].at[p, rows(((x + i) % 4) * 32, 32, 32)]
                arrived(there, *slot(a, A_ZZ + i * 4 + (4 - j)))
        for d in NEAR_FIRST:
            there = panel[a].at[p, rows(128 + ((x - d + 4) % 4) * 32, 32, 32)]
            arrived(there, *slot(a, A_XX + j * 4 + d))

    first_sends(0)

    local[4].wait()

    def spread(m, _):
        for k in range(4):
            t = tails[pl.ds(k, 1), pl.ds(pl.multiple_of(m * 128, 128), 128)] - e_idx * (4 * SUB)
            t = jnp.broadcast_to(t, (128, 128)).T
            for i in range(8):
                to = rows(i % 2 * 128 + m // 2 * 32 + i // 2 % 2 * 16, 16, 16)
                tb[k, m % 2 * 2 + i // 4, to] = t[i * 16 : (i + 1) * 16]
        return 0

    lax.fori_loop(0, 8, spread, 0)
    relays(0)
    first_sends(1)
    local[5].wait()

    def add(ref, value, first):
        ref[...] = value if first else ref[...] + value

    def grad_tile(j, far, first):
        p = (z + j) % 4
        half = 1 - yh if far else yh
        es = rows(half * 2 * SUB, 2 * SUB, 2 * SUB)
        q = qp[p]
        e = ent[es]
        score = dot_nt(q, e)
        lane = lax.broadcasted_iota(I32, (PLANE, 128), 1)
        label = []
        for b in range(2 * SUB // 128):
            ids = lane + (half * 2 * SUB + b * 128)
            hit = tb[0, p] == ids
            for k in range(1, 4):
                hit = hit | (tb[k, p] == ids)
            label.append(jnp.where(hit, 1.0, 0.0).astype(F32))
        label = jnp.concatenate(label, axis=1)
        prob = 1.0 / (1.0 + jnp.exp(-score))
        w[half, p] = prob * (1.0 - prob)
        ugrad = (prob - label).astype(BF16)
        add(qacc.at[GRAD, p], dot_nn(ugrad, e), far)
        add(eacc.at[GRAD, es], dot_tn(ugrad, q), first)

    def gnvp_tile(j, far, first):
        p = (z + j) % 4
        half = 1 - yh if far else yh
        es = rows(half * 2 * SUB, 2 * SUB, 2 * SUB)
        q = qp[p]
        e = ent[es]
        dscore = dot_nt(
            jnp.concatenate([dqp[p], q], axis=1), jnp.concatenate([e, ett[es]], axis=1)
        )
        uhess = (w[half, p] * dscore).astype(BF16)
        add(qacc.at[GNVP, p], dot_nn(uhess, e), far)
        add(eacc.at[GNVP, es], dot_tn(uhess, q), first)

    far_other = (1 - yh) * 2 + 1 - c
    far_same = (1 - yh) * 2 + c
    near_other = yh * 2 + 1 - c
    near_same = yh * 2 + c

    def to_core(k, i, s):
        for b in (0, 1):
            send(
                eacc.at[k, rows(s * SUB + b * 256, 256, 256)],
                drecv.at[k, i, pl.ds(b * 256, 256)],
                dsend.at[k, i, b],
                drsem.at[k, i, b],
                pcore,
            )

    def to_far(k):
        for b in (0, 1):
            here = drecv.at[k, 0, pl.ds(b * 256, 256)]
            arrived(here, dsend.at[k, 0, b], drsem.at[k, 0, b])
            value = eacc[k, rows(far_same * SUB + b * 256, 256, 256)] + here[...]
            quantize(value, csend.at[k, b], cssend.at[k, b])
            send(csend.at[k, b], crecv.at[k, b], cs_sem.at[k, b], cr_sem.at[k, b], phi)
            send(cssend.at[k, b], csrecv.at[k, b], css_sem.at[k, b], csr_sem.at[k, b], phi)

    def finish_entities(k, out):
        for b in (0, 1):
            here = drecv.at[k, 1, pl.ds(b * 256, 256)]
            arrived(here, dsend.at[k, 1, b], drsem.at[k, 1, b])
            arrived(csrecv.at[k, b], css_sem.at[k, b], csr_sem.at[k, b])
            arrived(crecv.at[k, b], cs_sem.at[k, b], cr_sem.at[k, b])
            out[pl.ds(b * 256, 256)] = (
                eacc[k, rows(near_same * SUB + b * 256, 256, 256)]
                + here[...]
                + dequantize(crecv.at[k, b], csrecv.at[k, b])
            )

    def to_1(k, j):
        p = (z + j) % 4
        quantize(qacc[k, p], bq.at[k, j], bqs.at[k, j])
        if j:
            send(bqs.at[k, j], br0s.at[k, j], b0s_ss.at[k, j], b0s_rs.at[k, j], pz(j))
            here = bq.at[k, j, pl.ds(0, 128)]
            send(here, br0.at[k, j], b0_ss.at[k, j], b0_rs.at[k, j], pz(j))
        for d in NEAR_FIRST:
            send(bqs.at[k, j], br1s.at[k, j, d], b1s_ss.at[k, j, d], b1s_rs.at[k, j, d], px(d))
            here = bq.at[k, j, rows(128 + ((x + d) % 4) * 32, 32, 32)]
            send(here, br1.at[k, j, d], b1_ss.at[k, j, d], b1_rs.at[k, j, d], px(d))

    def to_2(k):
        total = qacc[k, z, pl.ds(0, 128)]
        for j in NEAR_FIRST:
            arrived(br0s.at[k, j], b0s_ss.at[k, j], b0s_rs.at[k, j])
            arrived(br0.at[k, j], b0_ss.at[k, j], b0_rs.at[k, j])
            total = total + dequantize(br0.at[k, j], br0s.at[k, j])
        b2s[k, 0] = total
        quantize(total, b2q.at[k, 0], b2qs.at[k, 0])
        for d in NEAR_FIRST:
            send(b2qs.at[k, 0], b2rs.at[k, d], b2s_ss.at[k, d], b2s_rs.at[k, d], px(d))
            here = b2q.at[k, 0, rows(((x + d) % 4) * 32, 32, 32)]
            send(here, b2r.at[k, d], b2_ss.at[k, d], b2_rs.at[k, d], px(d))
        for j in (2, 1, 3, 0):
            total = qacc[k, (z + j) % 4, rows(128 + x * 32, 32, 32)]
            for d in NEAR_FIRST:
                arrived(br1s.at[k, j, d], b1s_ss.at[k, j, d], b1s_rs.at[k, j, d])
                arrived(br1.at[k, j, d], b1_ss.at[k, j, d], b1_rs.at[k, j, d])
                total = total + dequantize(br1.at[k, j, d], br1s.at[k, j, d])
            b2s[k, 1, pl.ds(j * 32, 32)] = total
        quantize(b2s[k, 1], b2q.at[k, 1], b2qs.at[k, 1])
        for j in NEAR_FIRST:
            i = 4 + j
            send(b2qs.at[k, 1], b2rs.at[k, i], b2s_ss.at[k, i], b2s_rs.at[k, i], pz(j))
            here = b2q.at[k, 1, pl.ds(j * 32, 32)]
            send(here, b2r.at[k, i], b2_ss.at[k, i], b2_rs.at[k, i], pz(j))

    def to_3(k):
        for h in (0, 1):
            total = b2s[k, 0, rows(x * 32, 32, 32)] if h == 0 else b2s[k, 1, pl.ds(0, 32)]
            for d in NEAR_FIRST:
                i = h * 4 + d
                arrived(b2rs.at[k, i], b2s_ss.at[k, i], b2s_rs.at[k, i])
                arrived(b2r.at[k, i], b2_ss.at[k, i], b2_rs.at[k, i])
                total = total + dequantize(b2r.at[k, i], b2rs.at[k, i])
            b3s[k, h] = total
            here = b3s.at[k, h, rows((1 - yl) * 16, 16, 16)]
            send(here, b3r.at[k, h], b3_ss.at[k, h], b3_rs.at[k, h], py)

    def finish_queries(k, out):
        for h in (0, 1):
            arrived(b3r.at[k, h], b3_ss.at[k, h], b3_rs.at[k, h])
            out[pl.ds(h * 16, 16)] = b3s[k, h, rows(yl * 16, 16, 16)] + b3r[k, h]

    for j in (0,) + NEAR_FIRST:
        plane_arrived(0, j)
        grad_tile(j, True, j == 0)
    to_core(GRAD, 0, far_other)
    relays(1)
    grad_tile(2, False, True)
    to_far(GRAD)
    to_1(GRAD, 2)
    grad_tile(1, False, False)
    to_1(GRAD, 1)
    grad_tile(3, False, False)
    to_1(GRAD, 3)
    grad_tile(0, False, False)
    to_1(GRAD, 0)
    to_core(GRAD, 1, near_other)
    local[6].wait()
    for j in (0,) + NEAR_FIRST:
        plane_arrived(1, j)
        gnvp_tile(j, True, j == 0)
    to_core(GNVP, 0, far_other)
    gnvp_tile(2, False, True)
    to_1(GNVP, 2)
    to_far(GNVP)
    gnvp_tile(1, False, False)
    to_1(GNVP, 1)
    to_2(GRAD)
    gnvp_tile(3, False, False)
    to_1(GNVP, 3)
    gnvp_tile(0, False, False)
    to_1(GNVP, 0)
    to_core(GNVP, 1, near_other)
    to_3(GRAD)
    to_2(GNVP)
    finish_queries(GRAD, oqg)
    to_3(GNVP)
    finish_entities(GRAD, oeg)
    finish_queries(GNVP, oqh)
    finish_entities(GNVP, oeh)
    for cp in started:
        cp.wait_send()


def store(a, b, c, d, to_a, to_b, to_c, to_d, sem):
    copies = [
        pltpu.make_async_copy(src, dst, sem.at[i])
        for i, (src, dst) in enumerate(((a, to_a), (b, to_b), (c, to_c), (d, to_d)))
    ]
    for cp in copies:
        cp.start()
    for cp in copies:
        cp.wait()


def per_device(ent_emb, ent_tan, qry_emb, qry_tan, tails):
    any_space = pl.BlockSpec(memory_space=pl.ANY)
    vmem = pl.BlockSpec(memory_space=pltpu.VMEM)
    dma = pltpu.SemaphoreType.DMA
    outs = (
        jax.ShapeDtypeStruct((SUB, D), F32),
        jax.ShapeDtypeStruct((SUB, D), F32),
        jax.ShapeDtypeStruct((32, D), F32),
        jax.ShapeDtypeStruct((32, D), F32),
    )
    results = pl.pallas_call(
        kernel,
        out_shape=outs,
        in_specs=[pl.BlockSpec(memory_space=pltpu.HBM)] * 5,
        out_specs=[vmem] * 4,
        scratch_shapes=[
            pltpu.VMEM((4 * SUB, D), BF16),
            pltpu.VMEM((4 * SUB, D), BF16),
            pltpu.VMEM((4, PLANE, D), BF16),
            pltpu.VMEM((4, PLANE, D), BF16),
            pltpu.VMEM((4, 4 * PLANE), I32),
            pltpu.VMEM((4, 4, PLANE, 128), I32),
            pltpu.VMEM((2, 4, PLANE, 2 * SUB), F32),
            pltpu.VMEM((2, 4, PLANE, D), F32),
            pltpu.VMEM((2, 4 * SUB, D), F32),
            pltpu.VMEM((2, 2, SUB, D), F32),
            pltpu.VMEM((2, 2, 256, D), I16),
            pltpu.VMEM((2, 2, 256, D), I16),
            pltpu.VMEM((2, 2, 8, 128), F32),
            pltpu.VMEM((2, 2, 8, 128), F32),
            pltpu.VMEM((2, 4, PLANE, D), I16),
            pltpu.VMEM((2, 4, 8, 128), F32),
            pltpu.VMEM((2, 4, 128, D), I16),
            pltpu.VMEM((2, 4, 8, 128), F32),
            pltpu.VMEM((2, 4, 4, 32, D), I16),
            pltpu.VMEM((2, 4, 4, 8, 128), F32),
            pltpu.VMEM((2, 2, 128, D), F32),
            pltpu.VMEM((2, 2, 128, D), I16),
            pltpu.VMEM((2, 2, 8, 128), F32),
            pltpu.VMEM((2, 8, 32, D), I16),
            pltpu.VMEM((2, 8, 8, 128), F32),
            pltpu.VMEM((2, 2, 32, D), F32),
            pltpu.VMEM((2, 2, 16, D), F32),
            dma((7,)),
            dma((2, A_N)),
            dma((2, A_N)),
            dma((2, 2, 2)),
            dma((2, 2, 2)),
            dma((2, 2)),
            dma((2, 2)),
            dma((2, 2)),
            dma((2, 2)),
            dma((2, 4)),
            dma((2, 4)),
            dma((2, 4)),
            dma((2, 4)),
            dma((2, 4, 4)),
            dma((2, 4, 4)),
            dma((2, 4, 4)),
            dma((2, 4, 4)),
            dma((2, 8)),
            dma((2, 8)),
            dma((2, 8)),
            dma((2, 8)),
            dma((2, 2)),
            dma((2, 2)),
        ],
        compiler_params=pltpu.CompilerParams(
            collective_id=0, has_side_effects=True, vmem_limit_bytes=VMEM_LIMIT
        ),
    )(*[pltpu.with_memory_space_constraint(a, pltpu.HBM) for a in (ent_emb, ent_tan, qry_emb, qry_tan, tails.T)])
    return pl.pallas_call(
        store,
        out_shape=outs,
        in_specs=[vmem] * 4,
        out_specs=[any_space] * 4,
        scratch_shapes=[dma((4,))],
        compiler_params=pltpu.CompilerParams(vmem_limit_bytes=8 * 2**20),
    )(*results)


def solution(mesh):
    return jax.shard_map(
        per_device,
        mesh=mesh,
        in_specs=(
            P("ent", None),
            P("ent", None),
            P(("qry", "ent"), None),
            P(("qry", "ent"), None),
            P("qry", None),
        ),
        out_specs=(
            P(("ent", "qry"), None),
            P(("ent", "qry"), None),
            P(("qry", "ent"), None),
            P(("qry", "ent"), None),
        ),
        check_vma=False,
    )
```
